32 devices in a mesh: dp: 16 (over z, x, core), tensor: 2 (over y).
Axes of the slice: x: 2, y: 2, z: 4, core: 2. Of those that a mesh axis runs over, the one named last changes fastest.
Arguments:
- inputs: bfloat16 [16384, 768], P(('dp', 'tensor')), may hold values from -6 to 6
- teacher: bfloat16 [16384, 768], P(('dp', 'tensor')), may hold values from -6 to 6
- lengths: int32 [16], P('dp'), may hold values from 256 to 1024
- w_query: bfloat16 [768, 768], P(('tensor', 'dp')), may hold values from -0.3125 to 0.3125
- w_key: bfloat16 [768, 768], P(('tensor', 'dp')), may hold values from -0.3125 to 0.3125
- w_value: bfloat16 [768, 768], P(('tensor', 'dp')), may hold values from -0.21875 to 0.21875
- w_out: bfloat16 [768, 768], P(('tensor', 'dp')), may hold values from -1.25 to 1.25
- w_up: bfloat16 [3072, 768], P(('tensor', 'dp')), may hold values from -0.21875 to 0.21875
- w_down: bfloat16 [3072, 768], P(('tensor', 'dp')), may hold values from -0.21875 to 0.21875
- b_query: float32 [768], replicated, may hold values from -3 to 3
- b_value: float32 [768], replicated, may hold values from -1.25 to 1.25
- b_out: float32 [768], replicated, may hold values from -1.75 to 1.75
- b_up: float32 [3072], replicated, may hold values from -3 to 3
- b_down: float32 [768], replicated, may hold values from -1.75 to 1.75
- gain_one: float32 [768], replicated, may hold values from 0.5 to 1.5
- shift_one: float32 [768], replicated, may hold values from -1.75 to 1.75
- gain_two: float32 [768], replicated, may hold values from 0.5 to 1.5
- shift_two: float32 [768], replicated, may hold values from -1.75 to 1.75
- z_head: float32 [12], replicated, may hold values from 0.4 to 1
- z_mha: float32 [1], replicated, may hold values from 0.4 to 1
- z_hidden: float32 [768], replicated, may hold values from 0.4 to 1
- z_int: float32 [3072], replicated, may hold values from 0.4 to 1
- z_ffn: float32 [1], replicated, may hold values from 0.4 to 1
Outputs:
- layer_out: float32 [16384, 768], P(('dp', 'tensor'))
- loss_value: float32 [1], replicated
- grad_inputs: float32 [16384, 768], P(('dp', 'tensor'))
- grad_w_query: float32 [768, 768], P(('tensor', 'dp'))
- grad_w_key: float32 [768, 768], P(('tensor', 'dp'))
- grad_w_value: float32 [768, 768], P(('tensor', 'dp'))
- grad_w_out: float32 [768, 768], P(('tensor', 'dp'))
- grad_w_up: float32 [3072, 768], P(('tensor', 'dp'))
- grad_w_down: float32 [3072, 768], P(('tensor', 'dp'))
- grad_b_query: float32 [768], replicated
- grad_b_value: float32 [768], replicated
- grad_b_out: float32 [768], replicated
- grad_b_up: float32 [3072], replicated
- grad_b_down: float32 [768], replicated
- grad_gain_one: float32 [768], replicated
- grad_shift_one: float32 [768], replicated
- grad_gain_two: float32 [768], replicated
- grad_shift_two: float32 [768], replicated
- grad_z_head: float32 [12], replicated
- grad_z_mha: float32 [1], replicated
- grad_z_hidden: float32 [768], replicated
- grad_z_int: float32 [3072], replicated
- grad_z_ffn: float32 [1], replicated
The draws below stay inside these ranges and needn't reach their ends.
All inputs are finite; a program needn't handle non-finite values.
Results may differ from the reference program's by a relative error of at most 0.013.
The reference program's roundings to bfloat16 on the way count: a program that leaves them out, or rounds other values in their place, can miss the bound.
Values may be sent and summed in bfloat16 or wider, within the bound.
A program may use at most 192 MiB of HBM per device.

```python
import math
import jax
import jax.numpy as jnp
from jax import lax

D = 768
HEADS = 12
FF = 3072
SEQ = 1024
SEQS_DEV = 1
HEAD_DIM = 64
SEQS = 16
TOKENS = 16384
N_DP = 16


def set_ends(drawn, key, low, largest):
    place = [jax.random.randint(jax.random.fold_in(key, axis), (), 0, length) for axis, length in enumerate(drawn.shape)]
    widest = drawn.shape.index(max(drawn.shape))
    neighbour = place[:widest] + [(place[widest] + 1) % drawn.shape[widest]] + place[widest + 1:]
    return drawn.at[tuple(place)].set(low).at[tuple(neighbour)].set(largest)


def shard_levels(key, shape, pieces, least, top_value):
    loudness = 1.0
    for dim, parts in pieces:
        draws = jax.random.uniform(jax.random.fold_in(jax.random.fold_in(key, 6), dim), (parts,), jnp.float32, least / len(pieces), top_value / len(pieces))
        loudness = loudness * jnp.repeat(jnp.exp(draws), shape[dim] // parts).reshape((-1,) + (1,) * (len(shape) - 1 - dim))
    return loudness


def normal_values(key, dims, spread, reach, split=(), held_as=jnp.bfloat16):
    gain = shard_levels(key, dims, split, -0.22, 0.18) if split else 1.0
    array = jax.random.normal(key, dims, jnp.float32) * spread * gain
    return jnp.minimum(jnp.maximum(array, -reach), reach).astype(held_as)


def setup_inputs(seed: int = 0) -> dict:
    streams_of = jax.random.split(jax.random.key(seed), 24)
    inputs = normal_values(streams_of[0], (TOKENS, D), 1.0, 6.0, ((0, 32),))
    teacher = normal_values(streams_of[1], (TOKENS, D), 1.0, 6.0, ((0, 32),))
    lengths = set_ends(jax.random.randint(streams_of[2], (SEQS,), SEQ // 4, SEQ + 1), jax.random.fold_in(streams_of[2], 1), SEQ // 4, SEQ).astype(jnp.int32)
    w_query = normal_values(streams_of[3], (D, D), (D // 2) ** -0.5, 0.3125, ((0, 32),))
    w_key = normal_values(streams_of[4], (D, D), (D // 2) ** -0.5, 0.3125, ((0, 32),))
    w_value = normal_values(streams_of[5], (D, D), D ** -0.5, 0.21875, ((0, 32),))
    w_out = normal_values(streams_of[6], (D, D), (D // 32) ** -0.5, 1.25, ((0, 32),))
    w_up = normal_values(streams_of[7], (FF, D), D ** -0.5, 0.21875, ((0, 32),))
    w_down = normal_values(streams_of[8], (FF, D), (FF // 4) ** -0.5, 0.21875, ((0, 32),))
    b_query = normal_values(streams_of[9], (D,), 0.5, 3.0, (), jnp.float32)
    b_value = normal_values(streams_of[10], (D,), 0.2, 1.25, (), jnp.float32)
    b_out = normal_values(streams_of[11], (D,), 0.3, 1.75, (), jnp.float32)
    b_up = normal_values(streams_of[12], (FF,), 0.5, 3.0, (), jnp.float32)
    b_down = normal_values(streams_of[13], (D,), 0.3, 1.75, (), jnp.float32)
    gain_one = jnp.clip(1.0 + 0.1 * jax.random.normal(streams_of[14], (D,), jnp.float32), 0.5, 1.5)
    shift_one = normal_values(streams_of[15], (D,), 0.3, 1.75, (), jnp.float32)
    gain_two = jnp.clip(1.0 + 0.1 * jax.random.normal(streams_of[16], (D,), jnp.float32), 0.5, 1.5)
    shift_two = normal_values(streams_of[17], (D,), 0.3, 1.75, (), jnp.float32)
    z_head = jnp.clip(jax.random.uniform(streams_of[18], (HEADS,), jnp.float32, 0.4, 1.0), 0.4, 1.0)
    z_mha = jnp.clip(jax.random.uniform(streams_of[19], (1,), jnp.float32, 0.4, 1.0), 0.4, 1.0)
    z_hidden = jnp.clip(jax.random.uniform(streams_of[20], (D,), jnp.float32, 0.4, 1.0), 0.4, 1.0)
    z_int = jnp.clip(jax.random.uniform(streams_of[21], (FF,), jnp.float32, 0.4, 1.0), 0.4, 1.0)
    z_ffn = jnp.clip(jax.random.uniform(streams_of[22], (1,), jnp.float32, 0.4, 1.0), 0.4, 1.0)
    return dict(inputs=inputs, teacher=teacher, lengths=lengths, w_query=w_query, w_key=w_key, w_value=w_value, w_out=w_out, w_up=w_up, w_down=w_down, b_query=b_query, b_value=b_value, b_out=b_out, b_up=b_up, b_down=b_down, gain_one=gain_one, shift_one=shift_one, gain_two=gain_two, shift_two=shift_two, z_head=z_head, z_mha=z_mha, z_hidden=z_hidden, z_int=z_int, z_ffn=z_ffn)


@jax.custom_vjp
def low(v):
    return lax.optimization_barrier(v.astype(jnp.bfloat16)).astype(jnp.float32)

@jax.custom_vjp
def low_back(v):
    return v

def low_keep(v):
    return (low(v), None)

def low_pass(kept, grad):
    return (grad,)

def back_keep(v):
    return (v, None)

def back_low(kept, grad):
    return (low(grad),)
low.defvjp(low_keep, low_pass)
low_back.defvjp(back_keep, back_low)
highest = lax.Precision.HIGHEST
epsilon = 1e-12

def norm_rows(summed, gain_vec, shift_vec):
    average = lax.optimization_barrier(jnp.mean(summed, axis=-1, keepdims=True))
    centered = summed - average
    variance = lax.optimization_barrier(jnp.mean(centered * centered, axis=-1, keepdims=True))
    return centered * lax.rsqrt(variance + epsilon) * gain_vec + shift_vec

def matmul_high(left, right):
    return jnp.dot(left, right, precision=highest)

def layer(weights_all, source, valid):
    w_query, w_key, w_value, w_out, w_up, w_down, b_query, b_value, b_out, b_up, b_down, gain_one, shift_one, gain_two, shift_two, z_head, z_mha, z_hidden, z_int, z_ffn = weights_all
    softmax_scale = 1.0 / math.sqrt(HEAD_DIM)
    group_rows = source.shape[0]
    seq_count = group_rows // SEQ
    query = low(low_back(matmul_high(source, w_query.T) + b_query) * softmax_scale)
    keys = low(low_back(matmul_high(source, w_key.T)))
    values = low(low_back(matmul_high(source, w_value.T) + b_value))
    query4 = query.reshape(seq_count, SEQ, HEADS, HEAD_DIM)
    keys4 = keys.reshape(seq_count, SEQ, HEADS, HEAD_DIM)
    values4 = values.reshape(seq_count, SEQ, HEADS, HEAD_DIM)
    scores = low_back(jnp.einsum('sqhd,skhd->shqk', query4, keys4, precision=highest))
    key_valid = valid.reshape(seq_count, 1, 1, SEQ)
    attention = low(jax.nn.softmax(jnp.where(key_valid, scores, -1e+30), axis=-1))
    heads_out = low_back(jnp.einsum('shqk,skhd->sqhd', attention, values4, precision=highest))
    context = low(heads_out * z_head[None, None, :, None]).reshape(group_rows, D)
    attn = low_back(matmul_high(context, w_out) + b_out)
    first_sum = source + z_mha * z_hidden * attn
    first_norm = norm_rows(first_sum, gain_one, shift_one)
    upper = low_back(matmul_high(low(first_norm), w_up.T) + b_up)
    hidden = low(jax.nn.gelu(upper, approximate=False) * z_int)
    down = low_back(matmul_high(hidden, w_down) + b_down)
    second_sum = first_norm + z_ffn * z_hidden * down
    return norm_rows(second_sum, gain_two, shift_two)

def reference(inputs, teacher, lengths, w_query, w_key, w_value, w_out, w_up, w_down, b_query, b_value, b_out, b_up, b_down, gain_one, shift_one, gain_two, shift_two, z_head, z_mha, z_hidden, z_int, z_ffn):
    group_rows = SEQS_DEV * SEQ
    valid_count = jnp.sum(lengths.astype(jnp.float32))
    weights_all = tuple((entry.astype(jnp.float32) for entry in (w_query, w_key, w_value, w_out, w_up, w_down, b_query, b_value, b_out, b_up, b_down, gain_one, shift_one, gain_two, shift_two, z_head, z_mha, z_hidden, z_int, z_ffn)))
    rows_all = inputs.reshape(N_DP, group_rows, D)
    targets = teacher.reshape(N_DP, group_rows, D)
    lens_all = lengths.reshape(N_DP, SEQS_DEV)
    sequence = (jnp.arange(group_rows) // SEQ).astype(jnp.int32)
    position = (jnp.arange(group_rows) % SEQ).astype(jnp.int32)
    loss_scale = D * TOKENS * 1.0

    def step(running, element):
        totals, loss_sum = running
        tok_rows, target, seq_lens = element
        valid = position < seq_lens[sequence]
        source = tok_rows.astype(jnp.float32)
        target_f = target.astype(jnp.float32)

        def objective(weights, source_rows):
            output = layer(weights, source_rows, valid)
            residue = output - target_f
            loss_term = jnp.sum(jnp.where(valid[:, None], residue * residue, 0.0)) / (D * valid_count)
            return (output, loss_term)
        (output, loss_term), pullback = jax.vjp(objective, weights_all, source)
        gradients, grad_rows = pullback((jnp.zeros_like(output), jnp.ones_like(loss_term) * loss_scale))
        totals = jax.tree.map(lambda left, right: left + right, totals, gradients)
        return ((totals, loss_sum + loss_term), (output, grad_rows))
    initial = jax.tree.map(jnp.zeros_like, weights_all)
    (totals, loss_sum), (outputs, grad_rows) = lax.scan(step, (initial, jnp.zeros((), jnp.float32)), (rows_all, targets, lens_all))
    return (outputs.reshape(TOKENS, D), loss_sum.reshape(1), grad_rows.reshape(TOKENS, D), totals[0], totals[1], totals[2], totals[3], totals[4], totals[5], totals[6], totals[7], totals[8], totals[9], totals[10], totals[11], totals[12], totals[13], totals[14], totals[15], totals[16], totals[17], totals[18], totals[19])
```

```python
import functools
import math

import jax
import jax.numpy as jnp
from jax import lax
from jax.experimental import pallas as pl
from jax.experimental.pallas import tpu as pltpu
from jax.sharding import PartitionSpec as P

D = 768
HEADS = 12
FF = 3072
SEQ = 1024


epsilon = 1e-12


def norm_rows(summed, gain_vec, shift_vec):
    average = jnp.mean(summed, axis=-1, keepdims=True)
    centered = summed - average
    variance = jnp.mean(centered * centered, axis=-1, keepdims=True)
    return centered * lax.rsqrt(variance + epsilon) * gain_vec + shift_vec


def gelu_exact(values):
    return jax.nn.gelu(values, approximate=False)


def times_plain(left, right):
    return jnp.dot(left, right, preferred_element_type=jnp.float32)


def times_trans(left, right):
    return lax.dot_general(
        left, right, (((1,), (1,)), ((), ())), preferred_element_type=jnp.float32
    )


def trans_times(left, right):
    return lax.dot_general(
        left, right, (((0,), (0,)), ((), ())), preferred_element_type=jnp.float32
    )


def gather_attn(w_query, w_key, w_value, w_out):
    return (
        lax.all_gather(w_query, "dp", axis=0, tiled=True),
        lax.all_gather(w_key, "dp", axis=0, tiled=True),
        lax.all_gather(w_value, "dp", axis=0, tiled=True),
        lax.all_gather(w_out, "dp", axis=0, tiled=True),
    )


def gather_ffn(w_up, w_down):
    return (
        lax.all_gather(w_up, "dp", axis=0, tiled=True),
        lax.all_gather(w_down, "dp", axis=0, tiled=True),
    )


def spread_into(local_vec, full_len, offset):
    return lax.dynamic_update_slice(jnp.zeros((full_len,), jnp.float32), local_vec, (offset,))


def on_device(
    inputs,
    teacher,
    lengths,
    w_query,
    w_key,
    w_value,
    w_out,
    w_up,
    w_down,
    b_query,
    b_value,
    b_out,
    b_up,
    b_down,
    gain_one,
    shift_one,
    gain_two,
    shift_two,
    z_head,
    z_mha,
    z_hidden,
    z_int,
    z_ffn,
):
    rows_own = inputs.shape[0]
    tensor_pos = lax.axis_index("tensor")
    tensor_count = lax.axis_size("tensor")
    group_rows = rows_own * tensor_count
    seq_count = group_rows // SEQ
    head_size = D // HEADS
    local_width = D // tensor_count
    heads_local = local_width // head_size
    units_local = FF // tensor_count
    qblock = min(512, SEQ)
    nblocks = SEQ // qblock
    softmax_scale = 1.0 / math.sqrt(head_size)
    positions = jnp.arange(group_rows, dtype=jnp.int32)
    seq_of_row = positions // SEQ
    picks = seq_of_row[:, None] == jnp.arange(seq_count, dtype=jnp.int32)[None, :]
    row_length = jnp.sum(jnp.where(picks, lengths[None, :], 0), axis=1)
    valid_group = positions % SEQ < row_length
    valid_own = lax.dynamic_slice_in_dim(valid_group, tensor_pos * rows_own, rows_own)
    head_start = tensor_pos * local_width
    unit_start = tensor_pos * units_local
    bias_query = lax.dynamic_slice_in_dim(b_query, head_start, local_width)
    bias_value = lax.dynamic_slice_in_dim(b_value, head_start, local_width)
    gate_heads = lax.dynamic_slice_in_dim(z_head, tensor_pos * heads_local, heads_local)
    bias_up = lax.dynamic_slice_in_dim(b_up, unit_start, units_local)
    gate_units = lax.dynamic_slice_in_dim(z_int, unit_start, units_local)
    wq_full, wk_full, wv_full, wo_full = gather_attn(w_query, w_key, w_value, w_out)
    x_group = lax.all_gather(inputs, "tensor", axis=0, tiled=True)
    query = ((times_trans(x_group, wq_full) + bias_query) * softmax_scale).astype(jnp.bfloat16)
    keys_b = times_trans(x_group, wk_full).astype(jnp.bfloat16)
    values_b = (times_trans(x_group, wv_full) + bias_value).astype(jnp.bfloat16)
    query5 = query.reshape(seq_count, nblocks, qblock, heads_local, head_size)
    keys4 = keys_b.reshape(seq_count, SEQ, heads_local, head_size)
    values4 = values_b.reshape(seq_count, SEQ, heads_local, head_size)
    valid2 = valid_group.reshape(seq_count, SEQ)

    def forward_seq(element):
        query_seq, keys_seq, values_seq, key_valid = element

        def forward_block(query_blk):
            scores = jnp.einsum(
                "qhd,khd->hqk", query_blk, keys_seq, preferred_element_type=jnp.float32
            )
            scores = jnp.where(key_valid[None, None, :], scores, -1e30)
            highest = jnp.max(scores, axis=-1, keepdims=True)
            exponent = jnp.exp(scores - highest)
            denominator = jnp.sum(exponent, axis=-1, keepdims=True)
            attention = (exponent / denominator).astype(jnp.bfloat16)
            context = jnp.einsum(
                "hqk,khd->qhd", attention, values_seq, preferred_element_type=jnp.float32
            )
            return (context, (highest + jnp.log(denominator))[..., 0])

        return lax.map(forward_block, query_seq)

    context_all, logsum_all = lax.map(forward_seq, (query5, keys4, values4, valid2))
    context_f = context_all.reshape(group_rows, heads_local, head_size)
    gated = (
        (context_f * gate_heads[None, :, None])
        .reshape(group_rows, local_width)
        .astype(jnp.bfloat16)
    )
    attn_out = (
        lax.psum_scatter(times_plain(gated, wo_full), "tensor", scatter_dimension=0, tiled=True)
        + b_out
    )
    branch_attn = z_mha * z_hidden
    first_sum = inputs.astype(jnp.float32) + branch_attn * attn_out
    first_norm = norm_rows(first_sum, gain_one, shift_one)
    y_group = lax.all_gather(first_norm.astype(jnp.bfloat16), "tensor", axis=0, tiled=True)
    wu_full, wd_full = gather_ffn(w_up, w_down)
    upper = times_trans(y_group, wu_full) + bias_up
    activated = gelu_exact(upper)
    hidden_b = (activated * gate_units).astype(jnp.bfloat16)
    down = (
        lax.psum_scatter(times_plain(hidden_b, wd_full), "tensor", scatter_dimension=0, tiled=True)
        + b_down
    )
    branch_ffn = z_ffn * z_hidden
    second_sum = first_norm + branch_ffn * down
    output = norm_rows(second_sum, gain_two, shift_two)
    residue = output - teacher.astype(jnp.float32)
    masked = jnp.where(valid_own[:, None], residue, 0.0)
    valid_count, square_sum = lax.psum(
        (jnp.sum(valid_own.astype(jnp.float32)), jnp.sum(masked * masked)), ("dp", "tensor")
    )
    loss_value = square_sum / (D * valid_count)
    tokens_all = group_rows * lax.axis_size("dp")
    grad_out = masked * (2.0 * tokens_all / valid_count)
    ffn_back = gather_ffn(w_up, w_down)
    attn_back = gather_attn(w_query, w_key, w_value, w_out)
    unused, pull_two = jax.vjp(norm_rows, second_sum, gain_two, shift_two)
    grad_second, grad_gain_two, grad_shift_two = pull_two(grad_out)
    grad_down = (grad_second * branch_ffn).astype(jnp.bfloat16)
    grad_z_ffn = jnp.sum(grad_second * z_hidden * down).reshape(1)
    hidden_part = jnp.sum(grad_second * z_ffn * down, axis=0)
    grad_b_down = jnp.sum(grad_down.astype(jnp.float32), axis=0)
    down_group = lax.all_gather(grad_down, "tensor", axis=0, tiled=True)
    grad_w_down = trans_times(hidden_b, down_group)
    grad_hidden = times_trans(down_group, ffn_back[1])
    grad_z_int_local = jnp.sum(grad_hidden * activated, axis=0)
    unused, gelu_pull = jax.vjp(gelu_exact, upper)
    grad_upper = gelu_pull(grad_hidden * gate_units)[0].astype(jnp.bfloat16)
    grad_b_up_local = jnp.sum(grad_upper.astype(jnp.float32), axis=0)
    grad_w_up = trans_times(grad_upper, y_group)
    grad_first_norm = grad_second + lax.psum_scatter(
        times_plain(grad_upper, ffn_back[0]), "tensor", scatter_dimension=0, tiled=True
    )
    unused, pull_one = jax.vjp(norm_rows, first_sum, gain_one, shift_one)
    grad_first, grad_gain_one, grad_shift_one = pull_one(grad_first_norm)
    grad_attn = (grad_first * branch_attn).astype(jnp.bfloat16)
    grad_z_mha = jnp.sum(grad_first * z_hidden * attn_out).reshape(1)
    hidden_part = hidden_part + jnp.sum(grad_first * z_mha * attn_out, axis=0)
    grad_b_out = jnp.sum(grad_attn.astype(jnp.float32), axis=0)
    attn_group = lax.all_gather(grad_attn, "tensor", axis=0, tiled=True)
    grad_w_out = trans_times(gated, attn_group)
    grad_gated = times_trans(attn_group, attn_back[3]).reshape(group_rows, heads_local, head_size)
    grad_z_head_local = jnp.sum(grad_gated * context_f, axis=(0, 2))
    grad_heads = (grad_gated * gate_heads[None, :, None]).astype(jnp.bfloat16)
    grad_heads5 = grad_heads.reshape(seq_count, nblocks, qblock, heads_local, head_size)

    def backward_seq(element):
        query_seq, keys_seq, values_seq, key_valid, grad_seq, logsum_seq = element
        initial = jnp.zeros((SEQ, heads_local, head_size), jnp.float32)

        def backward_block(running, block):
            keys_acc, values_acc = running
            query_blk, grad_blk, logsum_blk = block
            scores = jnp.einsum(
                "qhd,khd->hqk", query_blk, keys_seq, preferred_element_type=jnp.float32
            )
            scores = jnp.where(key_valid[None, None, :], scores, -1e30)
            attention = jnp.exp(scores - logsum_blk[..., None])
            attention_b = attention.astype(jnp.bfloat16)
            grad_attention = jnp.einsum(
                "qhd,khd->hqk", grad_blk, values_seq, preferred_element_type=jnp.float32
            )
            row_dots = jnp.sum(attention * grad_attention, axis=-1, keepdims=True)
            grad_scores = (attention * (grad_attention - row_dots)).astype(jnp.bfloat16)
            grad_query_blk = (
                softmax_scale
                * jnp.einsum(
                    "hqk,khd->qhd", grad_scores, keys_seq, preferred_element_type=jnp.float32
                )
            ).astype(jnp.bfloat16)
            keys_acc = keys_acc + jnp.einsum(
                "hqk,qhd->khd", grad_scores, query_blk, preferred_element_type=jnp.float32
            )
            values_acc = values_acc + jnp.einsum(
                "hqk,qhd->khd", attention_b, grad_blk, preferred_element_type=jnp.float32
            )
            return ((keys_acc, values_acc), grad_query_blk)

        (keys_acc, values_acc), grad_query_seq = lax.scan(
            backward_block, (initial, initial), (query_seq, grad_seq, logsum_seq)
        )
        return (grad_query_seq, keys_acc.astype(jnp.bfloat16), values_acc.astype(jnp.bfloat16))

    grad_query_all, grad_keys_all, grad_values_all = lax.map(
        backward_seq, (query5, keys4, values4, valid2, grad_heads5, logsum_all)
    )
    grad_query = grad_query_all.reshape(group_rows, local_width)
    grad_keys = grad_keys_all.reshape(group_rows, local_width)
    grad_values = grad_values_all.reshape(group_rows, local_width)
    grad_w_query = trans_times(grad_query, x_group)
    grad_w_key = trans_times(grad_keys, x_group)
    grad_w_value = trans_times(grad_values, x_group)
    grad_b_query_local = jnp.sum(grad_query.astype(jnp.float32), axis=0)
    grad_b_value_local = jnp.sum(grad_values.astype(jnp.float32), axis=0)
    part_query = times_plain(grad_query, attn_back[0])
    part_keys = times_plain(grad_keys, attn_back[1])
    part_values = times_plain(grad_values, attn_back[2])
    grad_inputs = grad_first + lax.psum_scatter(
        (part_query + part_keys + part_values).astype(jnp.bfloat16),
        "tensor",
        scatter_dimension=0,
        tiled=True,
    ).astype(jnp.float32)
    shard_wq, shard_wk, shard_wv, shard_wo, shard_wu, shard_wd = (
        lax.psum_scatter(grad_w_query, "dp", scatter_dimension=0, tiled=True),
        lax.psum_scatter(grad_w_key, "dp", scatter_dimension=0, tiled=True),
        lax.psum_scatter(grad_w_value, "dp", scatter_dimension=0, tiled=True),
        lax.psum_scatter(grad_w_out, "dp", scatter_dimension=0, tiled=True),
        lax.psum_scatter(grad_w_up, "dp", scatter_dimension=0, tiled=True),
        lax.psum_scatter(grad_w_down, "dp", scatter_dimension=0, tiled=True),
    )
    small_sums = lax.psum(
        (
            spread_into(grad_b_query_local, D, head_start),
            spread_into(grad_b_value_local, D, head_start),
            grad_b_out,
            spread_into(grad_b_up_local, FF, unit_start),
            grad_b_down,
            grad_gain_one,
            grad_shift_one,
            grad_gain_two,
            grad_shift_two,
            spread_into(grad_z_head_local, HEADS, tensor_pos * heads_local),
            grad_z_mha,
            hidden_part,
            spread_into(grad_z_int_local, FF, unit_start),
            grad_z_ffn,
        ),
        ("dp", "tensor"),
    )
    return (
        output,
        loss_value.reshape(1),
        grad_inputs,
        shard_wq,
        shard_wk,
        shard_wv,
        shard_wo,
        shard_wu,
        shard_wd,
        small_sums[0],
        small_sums[1],
        small_sums[2],
        small_sums[3],
        small_sums[4],
        small_sums[5],
        small_sums[6],
        small_sums[7],
        small_sums[8],
        small_sums[9],
        small_sums[10],
        small_sums[11],
        small_sums[12],
        small_sums[13],
    )


MESH = pl.DeviceIdType.MESH
F32 = jnp.float32
BF16 = jnp.bfloat16


def place():
    dp = lax.axis_index("dp")
    return dp // 4, (dp // 2) % 2, dp % 2, lax.axis_index("tensor")


def device(z, x, c, y):
    return ((z * 2 + x) * 2 + c, y)


def shard_of(z, x, c, y):
    return y * 16 + z * 4 + x * 2 + c


def remote(src, dst, send_sem, recv_sem, to):
    return pltpu.make_async_remote_copy(
        src_ref=src,
        dst_ref=dst,
        send_sem=send_sem,
        recv_sem=recv_sem,
        device_id=to,
        device_id_type=MESH,
    )


def greet(partners):
    barrier = pltpu.get_barrier_semaphore()
    for partner in partners:
        pl.semaphore_signal(barrier, inc=1, device_id=partner, device_id_type=MESH)
    pl.semaphore_wait(barrier, len(partners))


class Around:
    def __init__(self):
        z, x, c, y = place()
        self.z, self.x, self.c, self.y = z, x, c, y
        self.first = (x ^ c, y ^ (1 - c))
        self.second = (x ^ (1 - c), y ^ c)
        self.both = (1 - x, 1 - y)
        self.zs = [z ^ 1, z ^ 2, z ^ 3]
        self.sibling = device(z, x, 1 - c, y)
        self.by_first = device(z, self.first[0], c, self.first[1])
        self.by_second = device(z, self.second[0], c, self.second[1])
        self.by_z = [device(q, x, c, y) for q in self.zs]
        self.by_x = device(z, 1 - x, c, y)
        self.by_y = device(z, x, c, 1 - y)
        self.across = device(z, x, 1 - c, 1 - y)
        self.all = [self.sibling, self.by_first, self.by_second] + self.by_z + [self.across]


def gather_kernel(
    x_in, t_in, p1, p2, x_out, t_out, g1, g2, send1, send2, recv1, recv2, swap_s, swap_r, local
):
    d = Around()
    z, x, c, y = d.z, d.x, d.c, d.y
    greet(d.all)
    me = shard_of(z, x, c, y)
    swap_x = remote(x_in, x_out, swap_s.at[0], swap_r.at[0], d.across)
    swap_t = remote(t_in, t_out, swap_s.at[1], swap_r.at[1], d.across)
    keep_x = pltpu.make_async_copy(x_in, x_out, local.at[0])
    keep_t = pltpu.make_async_copy(t_in, t_out, local.at[1])

    @pl.when(c != y)
    def _():
        swap_x.start()

    @pl.when(c == y)
    def _():
        keep_x.start()
        keep_t.start()

    pending = []

    def group(own, full, send_sems, recv_sems, local_sem):
        count = [0]

        def send(src, shard, to):
            copy = remote(src, full.at[shard], send_sems.at[count[0]], recv_sems.at[shard], to)
            count[0] += 1
            copy.start()
            pending.append(copy)

        def got(shard, source):
            remote(
                full.at[shard], full.at[shard], send_sems.at[0], recv_sems.at[shard], source
            ).wait_recv()

        keep = pltpu.make_async_copy(own, full.at[me], local_sem)
        keep.start()
        send(own, me, d.by_second)
        send(own, me, d.by_first)
        for to in d.by_z:
            send(own, me, to)
        send(own, me, d.sibling)

        def from_first(q):
            shard = shard_of(q, d.first[0], c, d.first[1])
            got(shard, d.by_first)
            send(full.at[shard], shard, d.by_second)
            send(full.at[shard], shard, d.sibling)

        from_first(z)
        for q, source in zip(d.zs, d.by_z):
            shard = shard_of(q, x, c, y)
            got(shard, source)
            send(full.at[shard], shard, d.by_second)
            send(full.at[shard], shard, d.by_first)
            send(full.at[shard], shard, d.sibling)
        for q in d.zs:
            from_first(q)
        for xx, yy in (d.second, d.both):
            for q in [z] + d.zs:
                shard = shard_of(q, xx, c, yy)
                got(shard, d.by_second)
                send(full.at[shard], shard, d.sibling)

        def finish():
            keep.wait()
            for q in [z] + d.zs:
                for xx, yy in ((x, y), d.first, d.second, d.both):
                    got(shard_of(q, xx, 1 - c, yy), d.sibling)

        return finish

    finish1 = group(p1, g1, send1, recv1, local.at[2])

    @pl.when(c != y)
    def _():
        swap_t.start()

    finish2 = group(p2, g2, send2, recv2, local.at[3])
    finish1()
    finish2()
    for copy in pending:
        copy.wait_send()

    @pl.when(c != y)
    def _():
        swap_x.wait()
        swap_t.wait()

    @pl.when(c == y)
    def _():
        keep_x.wait()
        keep_t.wait()


def any_spec():
    return pl.BlockSpec(memory_space=pl.ANY)


def vmem_spec():
    return pl.BlockSpec(memory_space=pltpu.VMEM)


def shaped(shape, dtype):
    return jax.ShapeDtypeStruct(shape, dtype)


def dma(*shape):
    return pltpu.SemaphoreType.DMA(shape)


def gather_all(inputs, teacher, pack1, pack2):
    return pl.pallas_call(
        gather_kernel,
        out_shape=(
            shaped(inputs.shape, BF16),
            shaped(teacher.shape, BF16),
            shaped((32,) + pack1.shape, BF16),
            shaped((32,) + pack2.shape, BF16),
        ),
        in_specs=[any_spec()] * 4,
        out_specs=(any_spec(),) * 4,
        scratch_shapes=[dma(31), dma(31), dma(32), dma(32), dma(2), dma(2), dma(4)],
        compiler_params=pltpu.CompilerParams(collective_id=1, has_side_effects=True),
        name="gather_all",
    )(inputs, teacher, pack1, pack2)


def sum_into(target, sources, rows, step=24):
    def body(i, carry):
        span = pl.ds(pl.multiple_of(i * step, step), step)
        total = sources[0][span, :].astype(F32)
        for source in sources[1:]:
            total = total + source[span, :].astype(F32)
        target[span, :] = total.astype(target.dtype)
        return carry

    lax.fori_loop(0, rows // step, body, 0)


def scatter_kernel(
    part_f, part_q, out_in, grad_in, vec,
    sum_f, sum_q, out_swap, grad_swap, vec_sum,
    b0_f, b1_f, b2_f, b3_f, b0_q, b1_q, b2_q, b3_q, va, vb,
    s0_f, s1_f, s0_q, s1_q,
    r0_f, r1_f, r2_f, r3_f, r0_q, r1_q, r2_q, r3_q,
    vec_s, vec_r, swap_s, swap_r,
):
    d = Around()
    z, x, c, y = d.z, d.x, d.c, d.y
    greet(d.all)
    swap_o = remote(out_in, out_swap, swap_s.at[0], swap_r.at[0], d.across)
    swap_g = remote(grad_in, grad_swap, swap_s.at[1], swap_r.at[1], d.across)

    @pl.when(c != y)
    def _():
        swap_o.start()
        swap_g.start()

    pending = []
    order = d.zs + [z]

    def slot(q, xy):
        return q * 4 + xy[0] * 2 + xy[1]

    def to_sibling(part, b0, send_sems, recv_sems):
        count = 0
        for xy in (d.both, d.first, d.second, (x, y)):
            for q in order:
                at = slot(q, xy)
                copy = remote(
                    part.at[shard_of(q, xy[0], 1 - c, xy[1])],
                    b0.at[at],
                    send_sems.at[count],
                    recv_sems.at[at],
                    d.sibling,
                )
                count += 1
                copy.start()
                pending.append(copy)

    def got(buffer, at, sems, source):
        remote(buffer.at[at], buffer.at[at], s0_f.at[0], sems.at[at], source).wait_recv()

    to_sibling(part_f, b0_f, s0_f, r0_f)
    to_sibling(part_q, b0_q, s0_q, r0_q)

    def group(part, rows, b0, b1, b2, b3, send_sems, r0, r1, r2, r3, total):
        count = [0]

        def send(src, dst, sem, to):
            copy = remote(src, dst, send_sems.at[count[0]], sem, to)
            count[0] += 1
            copy.start()
            pending.append(copy)

        for j, xy in enumerate((d.both, d.second)):
            for q in order:
                at = slot(q, xy)
                got(b0, at, r0, d.sibling)
                sum_into(b0.at[at], [b0.at[at], part.at[shard_of(q, xy[0], c, xy[1])]], rows)
                send(b0.at[at], b1.at[j * 4 + q], r1.at[j * 4 + q], d.by_second)
        for q in order:
            at = slot(q, d.first)
            got(b0, at, r0, d.sibling)
            got(b1, q, r1, d.by_second)
            own = part.at[shard_of(q, d.first[0], c, d.first[1])]
            sum_into(b0.at[at], [b0.at[at], own, b1.at[q]], rows)
            send(b0.at[at], b2.at[q], r2.at[q], d.by_first)
        for i, q in enumerate(d.zs):
            at = slot(q, (x, y))
            got(b0, at, r0, d.sibling)
            got(b1, 4 + q, r1, d.by_second)
            got(b2, q, r2, d.by_first)
            own = part.at[shard_of(q, x, c, y)]
            sum_into(b0.at[at], [b0.at[at], own, b1.at[4 + q], b2.at[q]], rows)
            send(b0.at[at], b3.at[i], r3.at[i], d.by_z[i])

        def finish():
            at = slot(z, (x, y))
            got(b0, at, r0, d.sibling)
            got(b1, 4 + z, r1, d.by_second)
            got(b2, z, r2, d.by_first)
            for i in range(3):
                got(b3, i, r3, d.by_z[i])
            own = part.at[shard_of(z, x, c, y)]
            sum_into(
                total,
                [b0.at[at], own, b1.at[4 + z], b2.at[z], b3.at[0], b3.at[1], b3.at[2]],
                rows,
            )

        return finish

    finish_f = group(part_f, 216, b0_f, b1_f, b2_f, b3_f, s1_f, r0_f, r1_f, r2_f, r3_f, sum_f)
    finish_q = group(part_q, 72, b0_q, b1_q, b2_q, b3_q, s1_q, r0_q, r1_q, r2_q, r3_q, sum_q)
    va[0] = vec[...]
    for k, to in enumerate((d.sibling, d.by_x, d.by_y, d.by_z[0], d.by_z[1])):
        copy = remote(va.at[k], vb.at[k], vec_s.at[k], vec_r.at[k], to)
        copy.start()
        pending.append(copy)
        copy.wait_recv()
        if k < 4:
            va[k + 1] = va[k] + vb[k]
        else:
            vec_sum[...] = va[k] + vb[k]
    finish_f()
    finish_q()
    for copy in pending:
        copy.wait_send()

    @pl.when(c != y)
    def _():
        swap_o.wait()
        swap_g.wait()


def scatter_all(part_f, part_q, out_low, grad_low, vec):
    def buffers(rows):
        return [pltpu.VMEM((n, rows, D), BF16) for n in (16, 8, 4, 3)]

    return pl.pallas_call(
        scatter_kernel,
        out_shape=(
            shaped((216, D), F32),
            shaped((72, D), F32),
            shaped(out_low.shape, BF16),
            shaped(grad_low.shape, BF16),
            shaped(vec.shape, F32),
        ),
        in_specs=[vmem_spec(), vmem_spec(), any_spec(), any_spec(), vmem_spec()],
        out_specs=(vmem_spec(), vmem_spec(), any_spec(), any_spec(), vmem_spec()),
        scratch_shapes=buffers(216)
        + buffers(72)
        + [pltpu.VMEM((5,) + vec.shape, F32), pltpu.VMEM((5,) + vec.shape, F32)]
        + [dma(16), dma(15), dma(16), dma(15)]
        + [dma(16), dma(8), dma(4), dma(3), dma(16), dma(8), dma(4), dma(3)]
        + [dma(5), dma(5), dma(2), dma(2)],
        compiler_params=pltpu.CompilerParams(
            collective_id=2, has_side_effects=True, vmem_limit_bytes=60 << 20
        ),
        name="scatter_all",
    )(part_f, part_q, out_low, grad_low, vec)


def pair_kernel(own, both, send_sem, recv_sem, local):
    d = Around()
    greet([d.sibling])
    copy = remote(own, both.at[d.c], send_sem.at[0], recv_sem.at[0], d.sibling)
    copy.start()
    keep = pltpu.make_async_copy(own, both.at[d.c], local.at[0])
    keep.start()
    keep.wait()
    copy.wait_send()
    remote(own, both.at[1 - d.c], send_sem.at[0], recv_sem.at[0], d.sibling).wait_recv()


def pair(own):
    return pl.pallas_call(
        pair_kernel,
        out_shape=shaped((2,) + own.shape, own.dtype),
        in_specs=[any_spec()],
        out_specs=any_spec(),
        scratch_shapes=[dma(1), dma(1), dma(1)],
        compiler_params=pltpu.CompilerParams(collective_id=3, has_side_effects=True),
        name="pair",
    )(own)


def trade_kernel(parts, other, send_sem, recv_sem):
    d = Around()
    greet([d.sibling])
    copy = remote(parts.at[1 - d.c], other, send_sem.at[0], recv_sem.at[0], d.sibling)
    copy.start()
    copy.wait()


def trade(parts):
    return pl.pallas_call(
        trade_kernel,
        out_shape=shaped(parts.shape[1:], parts.dtype),
        in_specs=[any_spec()],
        out_specs=any_spec(),
        scratch_shapes=[dma(1), dma(1)],
        compiler_params=pltpu.CompilerParams(collective_id=4, has_side_effects=True),
        name="trade",
    )(parts)


def by_chip(
    inputs,
    teacher,
    lengths,
    w_query,
    w_key,
    w_value,
    w_out,
    w_up,
    w_down,
    b_query,
    b_value,
    b_out,
    b_up,
    b_down,
    gain_one,
    shift_one,
    gain_two,
    shift_two,
    z_head,
    z_mha,
    z_hidden,
    z_int,
    z_ffn,
):
    z, x, core, y = place()
    rows = inputs.shape[0]
    head_size = D // HEADS
    softmax_scale = 1.0 / math.sqrt(head_size)
    halves = jnp.concatenate([lengths // 32, lengths % 32]).astype(BF16)
    marks = jnp.pad(halves[None, :], ((0, 7), (0, D - 2)))
    pack1 = jnp.concatenate([w_query, w_key, w_value, marks], axis=0)
    pack2 = jnp.concatenate([w_up, w_down, w_out], axis=0)
    source, target, full1, full2 = gather_all(inputs, teacher, pack1, pack2)
    wq = full1[:, 0:24].reshape(D, D)
    wk = full1[:, 24:48].reshape(D, D)
    wv = full1[:, 48:72].reshape(D, D)
    wu = full2[:, 0:96].reshape(FF, D)
    wd = full2[:, 96:192].reshape(FF, D)
    wo = full2[:, 192:216].reshape(D, D)
    marks_all = full1[:16, 72, 0:2].astype(F32)
    lengths_all = marks_all[:, 0] * 32.0 + marks_all[:, 1]
    valid_count = jnp.sum(lengths_all)
    length = lengths_all[z * 4 + x * 2 + y]
    valid_keys = jnp.arange(SEQ, dtype=jnp.int32).astype(F32) < length
    positions = core * rows + jnp.arange(rows, dtype=jnp.int32)
    valid_own = positions.astype(F32) < length

    query = ((times_trans(source, wq) + b_query) * softmax_scale).astype(BF16)
    keys_own = times_trans(source, wk).astype(BF16)
    values_own = (times_trans(source, wv) + b_value).astype(BF16)
    kv = pair(jnp.concatenate([keys_own, values_own], axis=1)).reshape(SEQ, 2 * D)
    query3 = query.reshape(rows, HEADS, head_size)
    keys3 = kv[:, :D].reshape(SEQ, HEADS, head_size)
    values3 = kv[:, D:].reshape(SEQ, HEADS, head_size)
    scores = jnp.einsum("qhd,khd->hqk", query3, keys3, preferred_element_type=F32)
    scores = jnp.where(valid_keys[None, None, :], scores, -1e30)
    highest = jnp.max(scores, axis=-1, keepdims=True)
    exponent = jnp.exp(scores - highest)
    denominator = jnp.sum(exponent, axis=-1, keepdims=True)
    attention = exponent / denominator
    attention_b = attention.astype(BF16)
    context_f = jnp.einsum("hqk,khd->qhd", attention_b, values3, preferred_element_type=F32)
    gated = (context_f * z_head[None, :, None]).reshape(rows, D).astype(BF16)

    attn_out = times_plain(gated, wo) + b_out
    branch_attn = z_mha * z_hidden
    first_sum = source.astype(F32) + branch_attn * attn_out
    first_norm = norm_rows(first_sum, gain_one, shift_one)
    first_low = first_norm.astype(BF16)
    upper = times_trans(first_low, wu) + b_up
    activated = gelu_exact(upper)
    hidden_b = (activated * z_int).astype(BF16)
    down = times_plain(hidden_b, wd) + b_down
    branch_ffn = z_ffn * z_hidden
    second_sum = first_norm + branch_ffn * down
    output = norm_rows(second_sum, gain_two, shift_two)
    residue = output - target.astype(F32)
    masked = jnp.where(valid_own[:, None], residue, 0.0)
    square_sum = jnp.sum(masked * masked)
    tokens_all = rows * 32
    grad_out = masked * (2.0 * tokens_all / valid_count)
    unused, pull_two = jax.vjp(norm_rows, second_sum, gain_two, shift_two)
    grad_second, grad_gain_two, grad_shift_two = pull_two(grad_out)
    grad_down = (grad_second * branch_ffn).astype(BF16)
    grad_z_ffn = jnp.sum(grad_second * z_hidden * down).reshape(1)
    hidden_part = jnp.sum(grad_second * z_ffn * down, axis=0)
    grad_b_down = jnp.sum(grad_down.astype(F32), axis=0)
    grad_w_down = trans_times(hidden_b, grad_down).astype(BF16)
    grad_hidden = times_trans(grad_down, wd)
    grad_z_int = jnp.sum(grad_hidden * activated, axis=0)
    unused, gelu_pull = jax.vjp(gelu_exact, upper)
    grad_upper = gelu_pull(grad_hidden * z_int)[0].astype(BF16)
    grad_b_up = jnp.sum(grad_upper.astype(F32), axis=0)
    grad_w_up = trans_times(grad_upper, first_low).astype(BF16)
    grad_first_norm = grad_second + times_plain(grad_upper, wu)
    unused, pull_one = jax.vjp(norm_rows, first_sum, gain_one, shift_one)
    grad_first, grad_gain_one, grad_shift_one = pull_one(grad_first_norm)
    grad_attn = (grad_first * branch_attn).astype(BF16)
    grad_z_mha = jnp.sum(grad_first * z_hidden * attn_out).reshape(1)
    hidden_part = hidden_part + jnp.sum(grad_first * z_mha * attn_out, axis=0)
    grad_b_out = jnp.sum(grad_attn.astype(F32), axis=0)
    grad_w_out = trans_times(gated, grad_attn).astype(BF16)
    grad_gated = times_trans(grad_attn, wo).reshape(rows, HEADS, head_size)
    grad_z_head = jnp.sum(grad_gated * context_f, axis=(0, 2))
    grad_heads = (grad_gated * z_head[None, :, None]).astype(BF16)

    grad_attention = jnp.einsum(
        "qhd,khd->hqk", grad_heads, values3, preferred_element_type=F32
    )
    row_dots = jnp.sum(attention * grad_attention, axis=-1, keepdims=True)
    grad_scores = (attention * (grad_attention - row_dots)).astype(BF16)
    grad_query = (
        softmax_scale
        * jnp.einsum("hqk,khd->qhd", grad_scores, keys3, preferred_element_type=F32)
    ).astype(BF16).reshape(rows, D)
    grad_keys_part = jnp.einsum(
        "hqk,qhd->khd", grad_scores, query3, preferred_element_type=F32
    ).reshape(2, rows, D)
    grad_values_part = jnp.einsum(
        "hqk,qhd->khd", attention_b, grad_heads, preferred_element_type=F32
    ).reshape(2, rows, D)
    parts = jnp.concatenate([grad_keys_part, grad_values_part], axis=2)
    own_parts = lax.dynamic_index_in_dim(parts, core, 0, keepdims=False)
    grad_kv = (own_parts + trade(parts)).astype(BF16)
    grad_keys, grad_values = grad_kv[:, :D], grad_kv[:, D:]
    grad_w_query = trans_times(grad_query, source).astype(BF16)
    grad_w_key = trans_times(grad_keys, source).astype(BF16)
    grad_w_value = trans_times(grad_values, source).astype(BF16)
    grad_b_query = jnp.sum(grad_query.astype(F32), axis=0)
    grad_b_value = jnp.sum(grad_values.astype(F32), axis=0)
    grad_inputs = (
        grad_first
        + times_plain(grad_query, wq)
        + times_plain(grad_keys, wk)
        + times_plain(grad_values, wv)
    )
    part_f = jnp.concatenate(
        [
            grad_w_up.reshape(32, 96, D),
            grad_w_down.reshape(32, 96, D),
            grad_w_out.reshape(32, 24, D),
        ],
        axis=1,
    )
    part_q = jnp.concatenate(
        [
            grad_w_query.reshape(32, 24, D),
            grad_w_key.reshape(32, 24, D),
            grad_w_value.reshape(32, 24, D),
        ],
        axis=1,
    )
    pieces = (
        grad_b_query,
        grad_b_value,
        grad_b_out,
        grad_b_down,
        grad_gain_one,
        grad_shift_one,
        grad_gain_two,
        grad_shift_two,
        hidden_part,
        grad_b_up,
        grad_z_int,
        grad_z_head,
        grad_z_mha,
        grad_z_ffn,
        square_sum.reshape(1),
    )
    flat = jnp.concatenate(pieces)
    vec = jnp.pad(flat, (0, 104 * 128 - flat.shape[0])).reshape(104, 128)
    sum_f, sum_q, out_swap, grad_swap, vec_sum = scatter_all(
        part_f, part_q, output.astype(BF16), grad_inputs.astype(BF16), vec
    )
    total = vec_sum.reshape(-1)
    sums = []
    at = 0
    for piece in pieces:
        sums.append(total[at : at + piece.shape[0]])
        at += piece.shape[0]
    home = core == y
    layer_out = jnp.where(home, output, out_swap.astype(F32))
    grad_home = jnp.where(home, grad_inputs, grad_swap.astype(F32))
    (s_bq, s_bv, s_bo, s_bd, s_g1, s_s1, s_g2, s_s2, s_zh, s_bu, s_zi, s_hd, s_zm, s_zf, s_sq) = sums
    return (
        layer_out,
        s_sq / (D * valid_count),
        grad_home,
        sum_q[0:24],
        sum_q[24:48],
        sum_q[48:72],
        sum_f[192:216],
        sum_f[0:96],
        sum_f[96:192],
        s_bq,
        s_bv,
        s_bo,
        s_bu,
        s_bd,
        s_g1,
        s_s1,
        s_g2,
        s_s2,
        s_hd,
        s_zm,
        s_zh,
        s_zi,
        s_zf,
    )


def solution(mesh):
    sizes = (mesh.shape["dp"], mesh.shape["tensor"])
    return jax.shard_map(
        by_chip if sizes == (16, 2) else on_device,
        mesh=mesh,
        in_specs=(
            P(("dp", "tensor"), None),
            P(("dp", "tensor"), None),
            P("dp"),
            P(("tensor", "dp"), None),
            P(("tensor", "dp"), None),
            P(("tensor", "dp"), None),
            P(("tensor", "dp"), None),
            P(("tensor", "dp"), None),
            P(("tensor", "dp"), None),
            P(),
            P(),
            P(),
            P(),
            P(),
            P(),
            P(),
            P(),
            P(),
            P(),
            P(),
            P(),
            P(),
            P(),
        ),
        out_specs=(
            P(("dp", "tensor"), None),
            P(),
            P(("dp", "tensor"), None),
            P(("tensor", "dp"), None),
            P(("tensor", "dp"), None),
            P(("tensor", "dp"), None),
            P(("tensor", "dp"), None),
            P(("tensor", "dp"), None),
            P(("tensor", "dp"), None),
            P(),
            P(),
            P(),
            P(),
            P(),
            P(),
            P(),
            P(),
            P(),
            P(),
            P(),
            P(),
            P(),
            P(),
        ),
        check_vma=False,
    )
```

```python
import math

import jax
import jax.numpy as jnp
from jax import lax
from jax.experimental import pallas as pl
from jax.experimental.pallas import tpu as pltpu
from jax.sharding import PartitionSpec as P

D = 768
HEADS = 12
FF = 3072
SEQ = 1024


epsilon = 1e-12


def norm_rows(summed, gain_vec, shift_vec):
    average = jnp.mean(summed, axis=-1, keepdims=True)
    centered = summed - average
    variance = jnp.mean(centered * centered, axis=-1, keepdims=True)
    return centered * lax.rsqrt(variance + epsilon) * gain_vec + shift_vec


def gelu_exact(values):
    return jax.nn.gelu(values, approximate=False)


def times_plain(left, right):
    return jnp.dot(left, right, preferred_element_type=jnp.float32)


def times_trans(left, right):
    return lax.dot_general(
        left, right, (((1,), (1,)), ((), ())), preferred_element_type=jnp.float32
    )


def trans_times(left, right):
    return lax.dot_general(
        left, right, (((0,), (0,)), ((), ())), preferred_element_type=jnp.float32
    )


def gather_attn(w_query, w_key, w_value, w_out):
    return (
        lax.all_gather(w_query, "dp", axis=0, tiled=True),
        lax.all_gather(w_key, "dp", axis=0, tiled=True),
        lax.all_gather(w_value, "dp", axis=0, tiled=True),
        lax.all_gather(w_out, "dp", axis=0, tiled=True),
    )


def gather_ffn(w_up, w_down):
    return (
        lax.all_gather(w_up, "dp", axis=0, tiled=True),
        lax.all_gather(w_down, "dp", axis=0, tiled=True),
    )


def spread_into(local_vec, full_len, offset):
    return lax.dynamic_update_slice(jnp.zeros((full_len,), jnp.float32), local_vec, (offset,))


def on_device(
    inputs,
    teacher,
    lengths,
    w_query,
    w_key,
    w_value,
    w_out,
    w_up,
    w_down,
    b_query,
    b_value,
    b_out,
    b_up,
    b_down,
    gain_one,
    shift_one,
    gain_two,
    shift_two,
    z_head,
    z_mha,
    z_hidden,
    z_int,
    z_ffn,
):
    rows_own = inputs.shape[0]
    tensor_pos = lax.axis_index("tensor")
    tensor_count = lax.axis_size("tensor")
    group_rows = rows_own * tensor_count
    seq_count = group_rows // SEQ
    head_size = D // HEADS
    local_width = D // tensor_count
    heads_local = local_width // head_size
    units_local = FF // tensor_count
    qblock = min(512, SEQ)
    nblocks = SEQ // qblock
    softmax_scale = 1.0 / math.sqrt(head_size)
    positions = jnp.arange(group_rows, dtype=jnp.int32)
    seq_of_row = positions // SEQ
    picks = seq_of_row[:, None] == jnp.arange(seq_count, dtype=jnp.int32)[None, :]
    row_length = jnp.sum(jnp.where(picks, lengths[None, :], 0), axis=1)
    valid_group = positions % SEQ < row_length
    valid_own = lax.dynamic_slice_in_dim(valid_group, tensor_pos * rows_own, rows_own)
    head_start = tensor_pos * local_width
    unit_start = tensor_pos * units_local
    bias_query = lax.dynamic_slice_in_dim(b_query, head_start, local_width)
    bias_value = lax.dynamic_slice_in_dim(b_value, head_start, local_width)
    gate_heads = lax.dynamic_slice_in_dim(z_head, tensor_pos * heads_local, heads_local)
    bias_up = lax.dynamic_slice_in_dim(b_up, unit_start, units_local)
    gate_units = lax.dynamic_slice_in_dim(z_int, unit_start, units_local)
    wq_full, wk_full, wv_full, wo_full = gather_attn(w_query, w_key, w_value, w_out)
    x_group = lax.all_gather(inputs, "tensor", axis=0, tiled=True)
    query = ((times_trans(x_group, wq_full) + bias_query) * softmax_scale).astype(jnp.bfloat16)
    keys_b = times_trans(x_group, wk_full).astype(jnp.bfloat16)
    values_b = (times_trans(x_group, wv_full) + bias_value).astype(jnp.bfloat16)
    query5 = query.reshape(seq_count, nblocks, qblock, heads_local, head_size)
    keys4 = keys_b.reshape(seq_count, SEQ, heads_local, head_size)
    values4 = values_b.reshape(seq_count, SEQ, heads_local, head_size)
    valid2 = valid_group.reshape(seq_count, SEQ)

    def forward_seq(element):
        query_seq, keys_seq, values_seq, key_valid = element

        def forward_block(query_blk):
            scores = jnp.einsum(
                "qhd,khd->hqk", query_blk, keys_seq, preferred_element_type=jnp.float32
            )
            scores = jnp.where(key_valid[None, None, :], scores, -1e30)
            highest = jnp.max(scores, axis=-1, keepdims=True)
            exponent = jnp.exp(scores - highest)
            denominator = jnp.sum(exponent, axis=-1, keepdims=True)
            attention = (exponent / denominator).astype(jnp.bfloat16)
            context = jnp.einsum(
                "hqk,khd->qhd", attention, values_seq, preferred_element_type=jnp.float32
            )
            return (context, (highest + jnp.log(denominator))[..., 0])

        return lax.map(forward_block, query_seq)

    context_all, logsum_all = lax.map(forward_seq, (query5, keys4, values4, valid2))
    context_f = context_all.reshape(group_rows, heads_local, head_size)
    gated = (
        (context_f * gate_heads[None, :, None])
        .reshape(group_rows, local_width)
        .astype(jnp.bfloat16)
    )
    attn_out = (
        lax.psum_scatter(times_plain(gated, wo_full), "tensor", scatter_dimension=0, tiled=True)
        + b_out
    )
    branch_attn = z_mha * z_hidden
    first_sum = inputs.astype(jnp.float32) + branch_attn * attn_out
    first_norm = norm_rows(first_sum, gain_one, shift_one)
    y_group = lax.all_gather(first_norm.astype(jnp.bfloat16), "tensor", axis=0, tiled=True)
    wu_full, wd_full = gather_ffn(w_up, w_down)
    upper = times_trans(y_group, wu_full) + bias_up
    activated = gelu_exact(upper)
    hidden_b = (activated * gate_units).astype(jnp.bfloat16)
    down = (
        lax.psum_scatter(times_plain(hidden_b, wd_full), "tensor", scatter_dimension=0, tiled=True)
        + b_down
    )
    branch_ffn = z_ffn * z_hidden
    second_sum = first_norm + branch_ffn * down
    output = norm_rows(second_sum, gain_two, shift_two)
    residue = output - teacher.astype(jnp.float32)
    masked = jnp.where(valid_own[:, None], residue, 0.0)
    valid_count, square_sum = lax.psum(
        (jnp.sum(valid_own.astype(jnp.float32)), jnp.sum(masked * masked)), ("dp", "tensor")
    )
    loss_value = square_sum / (D * valid_count)
    tokens_all = group_rows * lax.axis_size("dp")
    grad_out = masked * (2.0 * tokens_all / valid_count)
    ffn_back = gather_ffn(w_up, w_down)
    attn_back = gather_attn(w_query, w_key, w_value, w_out)
    unused, pull_two = jax.vjp(norm_rows, second_sum, gain_two, shift_two)
    grad_second, grad_gain_two, grad_shift_two = pull_two(grad_out)
    grad_down = (grad_second * branch_ffn).astype(jnp.bfloat16)
    grad_z_ffn = jnp.sum(grad_second * z_hidden * down).reshape(1)
    hidden_part = jnp.sum(grad_second * z_ffn * down, axis=0)
    grad_b_down = jnp.sum(grad_down.astype(jnp.float32), axis=0)
    down_group = lax.all_gather(grad_down, "tensor", axis=0, tiled=True)
    grad_w_down = trans_times(hidden_b, down_group)
    grad_hidden = times_trans(down_group, ffn_back[1])
    grad_z_int_local = jnp.sum(grad_hidden * activated, axis=0)
    unused, gelu_pull = jax.vjp(gelu_exact, upper)
    grad_upper = gelu_pull(grad_hidden * gate_units)[0].astype(jnp.bfloat16)
    grad_b_up_local = jnp.sum(grad_upper.astype(jnp.float32), axis=0)
    grad_w_up = trans_times(grad_upper, y_group)
    grad_first_norm = grad_second + lax.psum_scatter(
        times_plain(grad_upper, ffn_back[0]), "tensor", scatter_dimension=0, tiled=True
    )
    unused, pull_one = jax.vjp(norm_rows, first_sum, gain_one, shift_one)
    grad_first, grad_gain_one, grad_shift_one = pull_one(grad_first_norm)
    grad_attn = (grad_first * branch_attn).astype(jnp.bfloat16)
    grad_z_mha = jnp.sum(grad_first * z_hidden * attn_out).reshape(1)
    hidden_part = hidden_part + jnp.sum(grad_first * z_mha * attn_out, axis=0)
    grad_b_out = jnp.sum(grad_attn.astype(jnp.float32), axis=0)
    attn_group = lax.all_gather(grad_attn, "tensor", axis=0, tiled=True)
    grad_w_out = trans_times(gated, attn_group)
    grad_gated = times_trans(attn_group, attn_back[3]).reshape(group_rows, heads_local, head_size)
    grad_z_head_local = jnp.sum(grad_gated * context_f, axis=(0, 2))
    grad_heads = (grad_gated * gate_heads[None, :, None]).astype(jnp.bfloat16)
    grad_heads5 = grad_heads.reshape(seq_count, nblocks, qblock, heads_local, head_size)

    def backward_seq(element):
        query_seq, keys_seq, values_seq, key_valid, grad_seq, logsum_seq = element
        initial = jnp.zeros((SEQ, heads_local, head_size), jnp.float32)

        def backward_block(running, block):
            keys_acc, values_acc = running
            query_blk, grad_blk, logsum_blk = block
            scores = jnp.einsum(
                "qhd,khd->hqk", query_blk, keys_seq, preferred_element_type=jnp.float32
            )
            scores = jnp.where(key_valid[None, None, :], scores, -1e30)
            attention = jnp.exp(scores - logsum_blk[..., None])
            attention_b = attention.astype(jnp.bfloat16)
            grad_attention = jnp.einsum(
                "qhd,khd->hqk", grad_blk, values_seq, preferred_element_type=jnp.float32
            )
            row_dots = jnp.sum(attention * grad_attention, axis=-1, keepdims=True)
            grad_scores = (attention * (grad_attention - row_dots)).astype(jnp.bfloat16)
            grad_query_blk = (
                softmax_scale
                * jnp.einsum(
                    "hqk,khd->qhd", grad_scores, keys_seq, preferred_element_type=jnp.float32
                )
            ).astype(jnp.bfloat16)
            keys_acc = keys_acc + jnp.einsum(
                "hqk,qhd->khd", grad_scores, query_blk, preferred_element_type=jnp.float32
            )
            values_acc = values_acc + jnp.einsum(
                "hqk,qhd->khd", attention_b, grad_blk, preferred_element_type=jnp.float32
            )
            return ((keys_acc, values_acc), grad_query_blk)

        (keys_acc, values_acc), grad_query_seq = lax.scan(
            backward_block, (initial, initial), (query_seq, grad_seq, logsum_seq)
        )
        return (grad_query_seq, keys_acc.astype(jnp.bfloat16), values_acc.astype(jnp.bfloat16))

    grad_query_all, grad_keys_all, grad_values_all = lax.map(
        backward_seq, (query5, keys4, values4, valid2, grad_heads5, logsum_all)
    )
    grad_query = grad_query_all.reshape(group_rows, local_width)
    grad_keys = grad_keys_all.reshape(group_rows, local_width)
    grad_values = grad_values_all.reshape(group_rows, local_width)
    grad_w_query = trans_times(grad_query, x_group)
    grad_w_key = trans_times(grad_keys, x_group)
    grad_w_value = trans_times(grad_values, x_group)
    grad_b_query_local = jnp.sum(grad_query.astype(jnp.float32), axis=0)
    grad_b_value_local = jnp.sum(grad_values.astype(jnp.float32), axis=0)
    part_query = times_plain(grad_query, attn_back[0])
    part_keys = times_plain(grad_keys, attn_back[1])
    part_values = times_plain(grad_values, attn_back[2])
    grad_inputs = grad_first + lax.psum_scatter(
        (part_query + part_keys + part_values).astype(jnp.bfloat16),
        "tensor",
        scatter_dimension=0,
        tiled=True,
    ).astype(jnp.float32)
    shard_wq, shard_wk, shard_wv, shard_wo, shard_wu, shard_wd = (
        lax.psum_scatter(grad_w_query, "dp", scatter_dimension=0, tiled=True),
        lax.psum_scatter(grad_w_key, "dp", scatter_dimension=0, tiled=True),
        lax.psum_scatter(grad_w_value, "dp", scatter_dimension=0, tiled=True),
        lax.psum_scatter(grad_w_out, "dp", scatter_dimension=0, tiled=True),
        lax.psum_scatter(grad_w_up, "dp", scatter_dimension=0, tiled=True),
        lax.psum_scatter(grad_w_down, "dp", scatter_dimension=0, tiled=True),
    )
    small_sums = lax.psum(
        (
            spread_into(grad_b_query_local, D, head_start),
            spread_into(grad_b_value_local, D, head_start),
            grad_b_out,
            spread_into(grad_b_up_local, FF, unit_start),
            grad_b_down,
            grad_gain_one,
            grad_shift_one,
            grad_gain_two,
            grad_shift_two,
            spread_into(grad_z_head_local, HEADS, tensor_pos * heads_local),
            grad_z_mha,
            hidden_part,
            spread_into(grad_z_int_local, FF, unit_start),
            grad_z_ffn,
        ),
        ("dp", "tensor"),
    )
    return (
        output,
        loss_value.reshape(1),
        grad_inputs,
        shard_wq,
        shard_wk,
        shard_wv,
        shard_wo,
        shard_wu,
        shard_wd,
        small_sums[0],
        small_sums[1],
        small_sums[2],
        small_sums[3],
        small_sums[4],
        small_sums[5],
        small_sums[6],
        small_sums[7],
        small_sums[8],
        small_sums[9],
        small_sums[10],
        small_sums[11],
        small_sums[12],
        small_sums[13],
    )


MESH = pl.DeviceIdType.MESH
F32 = jnp.float32
BF16 = jnp.bfloat16


def place():
    dp = lax.axis_index("dp")
    return dp // 4, (dp // 2) % 2, dp % 2, lax.axis_index("tensor")


def device(z, x, c, y):
    return ((z * 2 + x) * 2 + c, y)


def shard_of(z, x, c, y):
    return y * 16 + z * 4 + x * 2 + c


def remote(src, dst, send_sem, recv_sem, to):
    return pltpu.make_async_remote_copy(
        src_ref=src,
        dst_ref=dst,
        send_sem=send_sem,
        recv_sem=recv_sem,
        device_id=to,
        device_id_type=MESH,
    )


def greet(partners):
    barrier = pltpu.get_barrier_semaphore()
    for partner in partners:
        pl.semaphore_signal(barrier, inc=1, device_id=partner, device_id_type=MESH)
    pl.semaphore_wait(barrier, len(partners))


class Around:
    def __init__(self):
        z, x, c, y = place()
        self.z, self.x, self.c, self.y = z, x, c, y
        self.first = (x ^ c, y ^ (1 - c))
        self.second = (x ^ (1 - c), y ^ c)
        self.both = (1 - x, 1 - y)
        self.zs = [z ^ 1, z ^ 2, z ^ 3]
        self.sibling = device(z, x, 1 - c, y)
        self.by_first = device(z, self.first[0], c, self.first[1])
        self.by_second = device(z, self.second[0], c, self.second[1])
        self.by_z = [device(q, x, c, y) for q in self.zs]
        self.by_x = device(z, 1 - x, c, y)
        self.by_y = device(z, x, c, 1 - y)
        self.across = device(z, x, 1 - c, 1 - y)
        self.all = [self.sibling, self.by_first, self.by_second] + self.by_z + [self.across]


def gather_kernel(
    x_in, t_in, p1, p2, x_out, t_out, g1, g2, send1, send2, recv1, recv2, swap_s, swap_r, local
):
    d = Around()
    z, x, c, y = d.z, d.x, d.c, d.y
    greet(d.all)
    me = shard_of(z, x, c, y)
    swap_x = remote(x_in, x_out, swap_s.at[0], swap_r.at[0], d.across)
    swap_t = remote(t_in, t_out, swap_s.at[1], swap_r.at[1], d.across)
    keep_x = pltpu.make_async_copy(x_in, x_out, local.at[0])
    keep_t = pltpu.make_async_copy(t_in, t_out, local.at[1])

    @pl.when(c != y)
    def _():
        swap_x.start()

    @pl.when(c == y)
    def _():
        keep_x.start()
        keep_t.start()

    pending = []

    def group(own, full, send_sems, recv_sems, local_sem):
        count = [0]

        def send(src, shard, to):
            copy = remote(src, full.at[shard], send_sems.at[count[0]], recv_sems.at[shard], to)
            count[0] += 1
            copy.start()
            pending.append(copy)

        def got(shard, source):
            remote(
                full.at[shard], full.at[shard], send_sems.at[0], recv_sems.at[shard], source
            ).wait_recv()

        keep = pltpu.make_async_copy(own, full.at[me], local_sem)
        keep.start()
        send(own, me, d.by_second)
        send(own, me, d.by_first)
        for to in d.by_z:
            send(own, me, to)
        send(own, me, d.sibling)

        def from_first(q):
            shard = shard_of(q, d.first[0], c, d.first[1])
            got(shard, d.by_first)
            send(full.at[shard], shard, d.by_second)
            send(full.at[shard], shard, d.sibling)

        from_first(z)
        for q, source in zip(d.zs, d.by_z):
            shard = shard_of(q, x, c, y)
            got(shard, source)
            send(full.at[shard], shard, d.by_second)
            send(full.at[shard], shard, d.by_first)
            send(full.at[shard], shard, d.sibling)
        for q in d.zs:
            from_first(q)
        for xx, yy in (d.second, d.both):
            for q in [z] + d.zs:
                shard = shard_of(q, xx, c, yy)
                got(shard, d.by_second)
                send(full.at[shard], shard, d.sibling)

        def finish():
            keep.wait()
            for q in [z] + d.zs:
                for xx, yy in ((x, y), d.first, d.second, d.both):
                    got(shard_of(q, xx, 1 - c, yy), d.sibling)

        return finish

    finish1 = group(p1, g1, send1, recv1, local.at[2])

    @pl.when(c != y)
    def _():
        swap_t.start()

    finish2 = group(p2, g2, send2, recv2, local.at[3])
    finish1()
    finish2()
    for copy in pending:
        copy.wait_send()

    @pl.when(c != y)
    def _():
        swap_x.wait()
        swap_t.wait()

    @pl.when(c == y)
    def _():
        keep_x.wait()
        keep_t.wait()


def any_spec():
    return pl.BlockSpec(memory_space=pl.ANY)


def vmem_spec():
    return pl.BlockSpec(memory_space=pltpu.VMEM)


def shaped(shape, dtype):
    return jax.ShapeDtypeStruct(shape, dtype)


def dma(*shape):
    return pltpu.SemaphoreType.DMA(shape)


def gather_all(inputs, teacher, pack1, pack2):
    return pl.pallas_call(
        gather_kernel,
        out_shape=(
            shaped(inputs.shape, BF16),
            shaped(teacher.shape, BF16),
            shaped((32,) + pack1.shape, BF16),
            shaped((32,) + pack2.shape, BF16),
        ),
        in_specs=[any_spec()] * 4,
        out_specs=(any_spec(),) * 4,
        scratch_shapes=[dma(31), dma(31), dma(32), dma(32), dma(2), dma(2), dma(4)],
        compiler_params=pltpu.CompilerParams(collective_id=1, has_side_effects=True),
        name="gather_all",
    )(inputs, teacher, pack1, pack2)


def sum_into(target, sources, rows, step=24):
    def body(i, carry):
        span = pl.ds(pl.multiple_of(i * step, step), step)
        total = sources[0][span, :].astype(F32)
        for source in sources[1:]:
            total = total + source[span, :].astype(F32)
        target[span, :] = total.astype(target.dtype)
        return carry

    lax.fori_loop(0, rows // step, body, 0)


def scatter_kernel(
    part_f, part_q, out_in, grad_in, vec,
    sum_f, sum_q, out_swap, grad_swap, vec_sum,
    b0_f, b1_f, b2_f, b3_f, b0_q, b1_q, b2_q, b3_q, va, vb,
    s0_f, s1_f, s0_q, s1_q,
    r0_f, r1_f, r2_f, r3_f, r0_q, r1_q, r2_q, r3_q,
    vec_s, vec_r, swap_s, swap_r,
):
    d = Around()
    z, x, c, y = d.z, d.x, d.c, d.y
    greet(d.all)
    swap_o = remote(out_in, out_swap, swap_s.at[0], swap_r.at[0], d.across)
    swap_g = remote(grad_in, grad_swap, swap_s.at[1], swap_r.at[1], d.across)

    @pl.when(c != y)
    def _():
        swap_o.start()
        swap_g.start()

    pending = []
    order = d.zs + [z]

    def slot(q, xy):
        return q * 4 + xy[0] * 2 + xy[1]

    def to_sibling(part, b0, send_sems, recv_sems):
        count = 0
        for xy in (d.both, d.first, d.second, (x, y)):
            for q in order:
                at = slot(q, xy)
                copy = remote(
                    part.at[shard_of(q, xy[0], 1 - c, xy[1])],
                    b0.at[at],
                    send_sems.at[count],
                    recv_sems.at[at],
                    d.sibling,
                )
                count += 1
                copy.start()
                pending.append(copy)

    def got(buffer, at, sems, source):
        remote(buffer.at[at], buffer.at[at], s0_f.at[0], sems.at[at], source).wait_recv()

    to_sibling(part_f, b0_f, s0_f, r0_f)
    to_sibling(part_q, b0_q, s0_q, r0_q)

    def group(part, rows, b0, b1, b2, b3, send_sems, r0, r1, r2, r3, total):
        count = [0]

        def send(src, dst, sem, to):
            copy = remote(src, dst, send_sems.at[count[0]], sem, to)
            count[0] += 1
            copy.start()
            pending.append(copy)

        for j, xy in enumerate((d.both, d.second)):
            for q in order:
                at = slot(q, xy)
                got(b0, at, r0, d.sibling)
                sum_into(b0.at[at], [b0.at[at], part.at[shard_of(q, xy[0], c, xy[1])]], rows)
                send(b0.at[at], b1.at[j * 4 + q], r1.at[j * 4 + q], d.by_second)
        for q in order:
            at = slot(q, d.first)
            got(b0, at, r0, d.sibling)
            got(b1, q, r1, d.by_second)
            own = part.at[shard_of(q, d.first[0], c, d.first[1])]
            sum_into(b0.at[at], [b0.at[at], own, b1.at[q]], rows)
            send(b0.at[at], b2.at[q], r2.at[q], d.by_first)
        for i, q in enumerate(d.zs):
            at = slot(q, (x, y))
            got(b0, at, r0, d.sibling)
            got(b1, 4 + q, r1, d.by_second)
            got(b2, q, r2, d.by_first)
            own = part.at[shard_of(q, x, c, y)]
            sum_into(b0.at[at], [b0.at[at], own, b1.at[4 + q], b2.at[q]], rows)
            send(b0.at[at], b3.at[i], r3.at[i], d.by_z[i])

        def finish():
            at = slot(z, (x, y))
            got(b0, at, r0, d.sibling)
            got(b1, 4 + z, r1, d.by_second)
            got(b2, z, r2, d.by_first)
            for i in range(3):
                got(b3, i, r3, d.by_z[i])
            own = part.at[shard_of(z, x, c, y)]
            sum_into(
                total,
                [b0.at[at], own, b1.at[4 + z], b2.at[z], b3.at[0], b3.at[1], b3.at[2]],
                rows,
            )

        return finish

    finish_f = group(part_f, 216, b0_f, b1_f, b2_f, b3_f, s1_f, r0_f, r1_f, r2_f, r3_f, sum_f)
    finish_q = group(part_q, 72, b0_q, b1_q, b2_q, b3_q, s1_q, r0_q, r1_q, r2_q, r3_q, sum_q)
    va[0] = vec[...]
    for k, to in enumerate((d.sibling, d.by_x, d.by_y, d.by_z[0], d.by_z[1])):
        copy = remote(va.at[k], vb.at[k], vec_s.at[k], vec_r.at[k], to)
        copy.start()
        pending.append(copy)
        copy.wait_recv()
        if k < 4:
            va[k + 1] = va[k] + vb[k]
        else:
            vec_sum[...] = va[k] + vb[k]
    finish_f()
    finish_q()
    for copy in pending:
        copy.wait_send()

    @pl.when(c != y)
    def _():
        swap_o.wait()
        swap_g.wait()


def scatter_all(part_f, part_q, out_low, grad_low, vec):
    def buffers(rows):
        return [pltpu.VMEM((n, rows, D), BF16) for n in (16, 8, 4, 3)]

    return pl.pallas_call(
        scatter_kernel,
        out_shape=(
            shaped((216, D), F32),
            shaped((72, D), F32),
            shaped(out_low.shape, BF16),
            shaped(grad_low.shape, BF16),
            shaped(vec.shape, F32),
        ),
        in_specs=[vmem_spec(), vmem_spec(), any_spec(), any_spec(), vmem_spec()],
        out_specs=(vmem_spec(), vmem_spec(), any_spec(), any_spec(), vmem_spec()),
        scratch_shapes=buffers(216)
        + buffers(72)
        + [pltpu.VMEM((5,) + vec.shape, F32), pltpu.VMEM((5,) + vec.shape, F32)]
        + [dma(16), dma(15), dma(16), dma(15)]
        + [dma(16), dma(8), dma(4), dma(3), dma(16), dma(8), dma(4), dma(3)]
        + [dma(5), dma(5), dma(2), dma(2)],
        compiler_params=pltpu.CompilerParams(
            collective_id=2, has_side_effects=True, vmem_limit_bytes=60 << 20
        ),
        name="scatter_all",
    )(part_f, part_q, out_low, grad_low, vec)


ROWS = 512
SCALE = 0.125
BQ, BV, BO, BD, G1, S1, G2, S2, ZH, BU, ZI, SC = 0, 1, 2, 3, 4, 5, 6, 7, 8, 9, 13, 17
ROOT_HALF = math.sqrt(0.5)
DENSITY = 1.0 / math.sqrt(2.0 * math.pi)


def smem_spec():
    return pl.BlockSpec(memory_space=pltpu.SMEM)


def vmem(shape, dtype):
    return pltpu.VMEM(shape, dtype)


def stack_head(rows, half):
    blank = jnp.zeros_like(rows)
    return jnp.concatenate([rows, blank] if half == 0 else [blank, rows], axis=0)


def key_mask(mask, length):
    row = lax.broadcasted_iota(jnp.int32, mask.shape, 0)
    mask[...] = jnp.where(row < length, 0.0, -1e30)


def attend_kernel(
    length, z_head, x, w, bq, bv, q, qt, k, kt, v, ot, ctx, lse, vt, mask, send, recv
):
    d = Around()
    c = d.c
    greet([d.sibling])
    xv = x[...]

    def share(i, buf):
        copy = remote(buf.at[c], buf.at[c], send.at[i], recv.at[i], d.sibling)
        copy.start()
        return copy

    keys = times_trans(xv, w[1])
    k[c] = keys.astype(BF16)
    copies = [share(0, k)]
    kt[c] = keys.T.astype(BF16)
    copies.append(share(1, kt))
    values = times_trans(xv, w[2]) + bv[...]
    v[c] = values.astype(BF16)
    copies.append(share(2, v))
    vt[c] = values.T.astype(BF16)
    copies.append(share(3, vt))
    query = (times_trans(xv, w[0]) + bq[...]) * SCALE
    q[...] = query.astype(BF16)
    qt[...] = query.T.astype(BF16)
    key_mask(mask, length[0])
    for i, buf in enumerate((k, kt, v, vt)):
        remote(buf.at[1 - c], buf.at[1 - c], send.at[i], recv.at[i], d.sibling).wait_recv()
    for copy in copies:
        copy.wait_send()

    def pair_body(p, carry):
        lanes = pl.ds(pl.multiple_of(p * 128, 128), 128)
        kp = k[:, :, lanes].reshape(2 * ROWS, 128)
        off = jnp.concatenate([mask[...]] * 4, axis=1)
        for half in (0, 1):
            h = p * 2 + half
            span = pl.ds(pl.multiple_of(h * 64, 64), 64)
            s = times_plain(kp, stack_head(qt[span, :], half)) + off
            top = jnp.max(s, axis=0, keepdims=True)
            e = jnp.exp(s - top)
            den = jnp.sum(e, axis=0, keepdims=True)
            probs = (e * (1.0 / den)).astype(BF16)
            ot[span, :] = times_plain(vt[0, span, :], probs[:ROWS]) + times_plain(
                vt[1, span, :], probs[ROWS:]
            )
            lse[pl.ds(h, 1), :] = top + jnp.log(den)
        return carry

    lax.fori_loop(0, HEADS // 2, pair_body, 0)
    for h in range(HEADS):
        span = slice(h * 64, h * 64 + 64)
        ctx[:, span] = (ot[span, :] * z_head[h]).T.astype(BF16)


def attend(length, z_head, x, w, bq, bv):
    return pl.pallas_call(
        attend_kernel,
        out_shape=(
            shaped((ROWS, D), BF16),
            shaped((D, ROWS), BF16),
            shaped((2, ROWS, D), BF16),
            shaped((2, D, ROWS), BF16),
            shaped((2, ROWS, D), BF16),
            shaped((D, ROWS), F32),
            shaped((ROWS, D), BF16),
            shaped((HEADS, ROWS), F32),
        ),
        in_specs=[smem_spec()] * 2 + [vmem_spec()] * 4,
        out_specs=(vmem_spec(),) * 8,
        scratch_shapes=[vmem((2, D, ROWS), BF16), vmem((2 * ROWS, 128), F32), dma(4), dma(4)],
        compiler_params=pltpu.CompilerParams(
            collective_id=5, has_side_effects=True, vmem_limit_bytes=60 << 20
        ),
        name="attend",
    )(length, z_head, x, w, bq, bv)


def rows_loop(body, step=128):
    def run(i, carry):
        body(i * step, pl.ds(pl.multiple_of(i * step, step), step))
        return carry

    lax.fori_loop(0, ROWS // step, run, 0)


def col_sum(values):
    return jnp.sum(values, axis=0, keepdims=True)


def row_mean(values):
    return jnp.sum(values, axis=1, keepdims=True) * (1.0 / D)


def mid_kernel(
    length, count, zm, zf, z_head,
    x, t, ctx, ot, wo, wu, wd, bo, bu, bd, g1, s1, g2, s2, zh, zi,
    out, dwu, dwd, dwo, gfirst, g, gt, vec,
    attn, fn, xh1, r1, low, up, cdf, hid, gsec, gdown, acc,
):
    c = lax.axis_index("dp") % 2
    vec[...] = jnp.zeros_like(vec)
    lane = lax.broadcasted_iota(jnp.int32, (1, D), 1)

    def add(row, value):
        vec[row : row + 1, :] += value

    def add_scalar(at, value):
        vec[SC : SC + 1, :] += jnp.where(lane == at, value, 0.0)

    attn[...] = times_plain(ctx[...], wo[...]) + bo[...]
    ba = zm[0] * zh[...]
    bf = zf[0] * zh[...]

    def first(at, span):
        h = x[span, :].astype(F32) + ba * attn[span, :]
        cen = h - row_mean(h)
        r = lax.rsqrt(row_mean(cen * cen) + epsilon)
        xh = cen * r
        xh1[span, :] = xh
        r1[span, :] = jnp.broadcast_to(r, (128, 128))
        f = xh * g1[...] + s1[...]
        fn[span, :] = f
        low[span, :] = f.astype(BF16)

    rows_loop(first)
    acc[...] = jnp.zeros_like(acc)

    def unit_fwd(j, carry):
        units = pl.ds(pl.multiple_of(j * D, D), D)
        u = times_trans(low[...], wu[units, :]) + bu[:, units]
        up[:, units] = u
        cd = 0.5 * (1.0 + lax.erf(u * ROOT_HALF))
        cdf[:, units] = cd
        hv = (u * cd * zi[:, units]).astype(BF16)
        hid[:, units] = hv
        acc[...] += times_plain(hv, wd[units, :])
        return carry

    lax.fori_loop(0, FF // D, unit_fwd, 0)
    scale = (2.0 * 32 * ROWS) / count[0]

    def second(at, span):
        down = acc[span, :] + bd[...]
        h = fn[span, :] + bf * down
        cen = h - row_mean(h)
        r = lax.rsqrt(row_mean(cen * cen) + epsilon)
        xh = cen * r
        o = xh * g2[...] + s2[...]
        out[span, :] = o
        pos = lax.broadcasted_iota(jnp.int32, (128, D), 0) + (c * ROWS + at)
        res = jnp.where(pos < length[0], o - t[span, :].astype(F32), 0.0)
        add_scalar(14, jnp.sum(res * res))
        go = res * scale
        add(G2, col_sum(go * xh))
        add(S2, col_sum(go))
        e = go * g2[...]
        gs = r * (e - row_mean(e) - xh * row_mean(e * xh))
        gsec[span, :] = gs
        gd = (gs * bf).astype(BF16)
        gdown[span, :] = gd
        add(BD, col_sum(gd.astype(F32)))
        gsd = gs * down
        add_scalar(13, jnp.sum(gsd * zh[...]))
        add(ZH, col_sum(gsd * zf[0]))

    rows_loop(second)
    acc[...] = gsec[...]

    def unit_bwd(j, carry):
        units = pl.ds(pl.multiple_of(j * D, D), D)
        gh = times_trans(gdown[...], wd[units, :])
        u = up[:, units]
        cd = cdf[:, units]
        vec[pl.ds(ZI + j, 1), :] = col_sum(gh * (u * cd))
        gu = (gh * zi[:, units] * (cd + u * (DENSITY * jnp.exp(-0.5 * u * u)))).astype(BF16)
        vec[pl.ds(BU + j, 1), :] = col_sum(gu.astype(F32))
        acc[...] += times_plain(gu, wu[units, :])
        dwd[units, :] = trans_times(hid[:, units], gdown[...]).astype(BF16)
        dwu[units, :] = trans_times(gu, low[...]).astype(BF16)
        return carry

    lax.fori_loop(0, FF // D, unit_bwd, 0)

    def third(at, span):
        gf = acc[span, :]
        xh = xh1[span, :]
        add(G1, col_sum(gf * xh))
        add(S1, col_sum(gf))
        e = gf * g1[...]
        gr = r1[span, 0:1] * (e - row_mean(e) - xh * row_mean(e * xh))
        gfirst[span, :] = gr
        ga = (gr * ba).astype(BF16)
        low[span, :] = ga
        add(BO, col_sum(ga.astype(F32)))
        gra = gr * attn[span, :]
        add_scalar(12, jnp.sum(gra * zh[...]))
        add(ZH, col_sum(gra * zm[0]))

    rows_loop(third)
    dwo[...] = trans_times(ctx[...], low[...]).astype(BF16)
    gct = times_trans(wo[...], low[...])
    for h in range(HEADS):
        span = slice(h * 64, h * 64 + 64)
        block = gct[span, :]
        add_scalar(h, jnp.sum(block * ot[span, :]))
        gb = block * z_head[h]
        gt[span, :] = gb.astype(BF16)
        g[:, span] = gb.T.astype(BF16)


def mid(length, count, zm, zf, z_head, *arrays):
    return pl.pallas_call(
        mid_kernel,
        out_shape=(
            shaped((ROWS, D), F32),
            shaped((FF, D), BF16),
            shaped((FF, D), BF16),
            shaped((D, D), BF16),
            shaped((ROWS, D), F32),
            shaped((ROWS, D), BF16),
            shaped((D, ROWS), BF16),
            shaped((24, D), F32),
        ),
        in_specs=[smem_spec()] * 5 + [vmem_spec()] * len(arrays),
        out_specs=(vmem_spec(),) * 8,
        scratch_shapes=[
            vmem((ROWS, D), F32),
            vmem((ROWS, D), F32),
            vmem((ROWS, D), F32),
            vmem((ROWS, 128), F32),
            vmem((ROWS, D), BF16),
            vmem((ROWS, FF), F32),
            vmem((ROWS, FF), F32),
            vmem((ROWS, FF), BF16),
            vmem((ROWS, D), F32),
            vmem((ROWS, D), BF16),
            vmem((ROWS, D), F32),
        ],
        compiler_params=pltpu.CompilerParams(vmem_limit_bytes=63 << 20),
        name="mid",
    )(length, count, zm, zf, z_head, *arrays)


def back_kernel(
    length, x, w, q, qt, k, kt, v, g, gt, ot, lse, gfirst, vec_in,
    dw, gin, vec, dqt, dkp, dvp, mask, rk, rv, send, recv,
):
    d = Around()
    c = d.c
    greet([d.sibling])
    key_mask(mask, length[0])
    lane = lax.broadcasted_iota(jnp.int32, (ROWS, 128), 1)

    def pair_body(p, carry):
        lanes = pl.ds(pl.multiple_of(p * 128, 128), 128)
        kp = k[:, :, lanes].reshape(2 * ROWS, 128)
        vp = v[:, :, lanes].reshape(2 * ROWS, 128)
        qp = q[:, lanes]
        gp = g[:, lanes]
        off = jnp.concatenate([mask[...]] * 4, axis=1)
        zero = jnp.zeros_like(qp)
        dka = []
        dva = []
        for half in (0, 1):
            h = p * 2 + half
            span = pl.ds(pl.multiple_of(h * 64, 64), 64)
            mine = (lane >= 64) if half else (lane < 64)
            s = times_plain(kp, stack_head(qt[span, :], half)) + off
            probs = jnp.exp(s - lse[pl.ds(h, 1), :])
            gth = gt[span, :]
            gp_t = times_plain(vp, stack_head(gth, half))
            dots = col_sum(gth.astype(F32) * ot[span, :])
            ds = (probs * (gp_t - dots)).astype(BF16)
            dka.append(times_plain(ds, jnp.where(mine, qp, zero)))
            dva.append(times_plain(probs.astype(BF16), jnp.where(mine, gp, zero)))
            dq = times_plain(kt[0, span, :], ds[:ROWS]) + times_plain(kt[1, span, :], ds[ROWS:])
            dqt[span, :] = (dq * SCALE).astype(BF16)
        dkp[:, :, lanes] = (dka[0] + dka[1]).reshape(2, ROWS, 128)
        dvp[:, :, lanes] = (dva[0] + dva[1]).reshape(2, ROWS, 128)
        return carry

    lax.fori_loop(0, HEADS // 2, pair_body, 0)
    copies = [
        remote(dkp.at[1 - c], rk, send.at[0], recv.at[0], d.sibling),
        remote(dvp.at[1 - c], rv, send.at[1], recv.at[1], d.sibling),
    ]
    for copy in copies:
        copy.start()
    dw[0] = times_plain(dqt[...], x[...]).astype(BF16)
    dq = dqt[...].astype(F32).T
    vec[...] = vec_in[...]
    vec[BQ : BQ + 1, :] = col_sum(dq)
    total = gfirst[...] + times_plain(dq.astype(BF16), w[0])
    for copy in copies:
        copy.wait()
    dk = (dkp[c] + rk[...]).astype(BF16)
    dv = (dvp[c] + rv[...]).astype(BF16)
    vec[BV : BV + 1, :] = col_sum(dv.astype(F32))
    dw[1] = trans_times(dk, x[...]).astype(BF16)
    dw[2] = trans_times(dv, x[...]).astype(BF16)
    gin[...] = total + times_plain(dk, w[1]) + times_plain(dv, w[2])


def back(length, *arrays):
    return pl.pallas_call(
        back_kernel,
        out_shape=(shaped((3, D, D), BF16), shaped((ROWS, D), F32), shaped((24, D), F32)),
        in_specs=[smem_spec()] + [vmem_spec()] * len(arrays),
        out_specs=(vmem_spec(),) * 3,
        scratch_shapes=[
            vmem((D, ROWS), BF16),
            vmem((2, ROWS, D), F32),
            vmem((2, ROWS, D), F32),
            vmem((2 * ROWS, 128), F32),
            vmem((ROWS, D), F32),
            vmem((ROWS, D), F32),
            dma(2),
            dma(2),
        ],
        compiler_params=pltpu.CompilerParams(
            collective_id=6, has_side_effects=True, vmem_limit_bytes=63 << 20
        ),
        name="back",
    )(length, *arrays)


def by_chip(
    inputs,
    teacher,
    lengths,
    w_query,
    w_key,
    w_value,
    w_out,
    w_up,
    w_down,
    b_query,
    b_value,
    b_out,
    b_up,
    b_down,
    gain_one,
    shift_one,
    gain_two,
    shift_two,
    z_head,
    z_mha,
    z_hidden,
    z_int,
    z_ffn,
):
    z, x, core, y = place()
    halves = jnp.concatenate([lengths // 32, lengths % 32]).astype(BF16)
    marks = jnp.pad(halves[None, :], ((0, 7), (0, D - 2)))
    pack1 = jnp.concatenate([w_query, w_key, w_value, marks], axis=0)
    pack2 = jnp.concatenate([w_up, w_down, w_out], axis=0)
    source, target, full1, full2 = gather_all(inputs, teacher, pack1, pack2)
    wqkv = jnp.stack([full1[:, i * 24 : i * 24 + 24].reshape(D, D) for i in range(3)])
    wu = full2[:, 0:96].reshape(FF, D)
    wd = full2[:, 96:192].reshape(FF, D)
    wo = full2[:, 192:216].reshape(D, D)
    marks_all = full1[:16, 72, 0:2].astype(F32)
    lengths_all = marks_all[:, 0] * 32.0 + marks_all[:, 1]
    valid_count = jnp.sum(lengths_all).reshape(1)
    length = lengths_all[z * 4 + x * 2 + y].astype(jnp.int32).reshape(1)
    row = lambda a: a.reshape(1, -1)
    q, qt, k, kt, v, ot, ctx, lse = attend(
        length, z_head, source, wqkv, row(b_query), row(b_value)
    )
    output, dwu, dwd, dwo, gfirst, g, gt, vec = mid(
        length, valid_count, z_mha, z_ffn, z_head,
        source, target, ctx, ot, wo, wu, wd, row(b_out), row(b_up), row(b_down),
        row(gain_one), row(shift_one), row(gain_two), row(shift_two), row(z_hidden), row(z_int),
    )
    dw, grad_inputs, vec = back(
        length, source, wqkv, q, qt, k, kt, v, g, gt, ot, lse, gfirst, vec
    )
    part_f = jnp.concatenate(
        [dwu.reshape(32, 96, D), dwd.reshape(32, 96, D), dwo.reshape(32, 24, D)], axis=1
    )
    part_q = jnp.concatenate([dw[i].reshape(32, 24, D) for i in range(3)], axis=1)
    sum_f, sum_q, out_swap, grad_swap, sums = scatter_all(
        part_f, part_q, output.astype(BF16), grad_inputs.astype(BF16), vec
    )
    home = core == y
    layer_out = jnp.where(home, output, out_swap.astype(F32))
    grad_home = jnp.where(home, grad_inputs, grad_swap.astype(F32))
    return (
        layer_out,
        sums[SC, 14:15] / (D * valid_count),
        grad_home,
        sum_q[0:24],
        sum_q[24:48],
        sum_q[48:72],
        sum_f[192:216],
        sum_f[0:96],
        sum_f[96:192],
        sums[BQ],
        sums[BV],
        sums[BO],
        sums[BU : BU + 4].reshape(-1),
        sums[BD],
        sums[G1],
        sums[S1],
        sums[G2],
        sums[S2],
        sums[SC, 0:12],
        sums[SC, 12:13],
        sums[ZH],
        sums[ZI : ZI + 4].reshape(-1),
        sums[SC, 13:14],
    )


def solution(mesh):
    sizes = (mesh.shape["dp"], mesh.shape["tensor"])
    return jax.shard_map(
        by_chip if sizes == (16, 2) else on_device,
        mesh=mesh,
        in_specs=(
            P(("dp", "tensor"), None),
            P(("dp", "tensor"), None),
            P("dp"),
            P(("tensor", "dp"), None),
            P(("tensor", "dp"), None),
            P(("tensor", "dp"), None),
            P(("tensor", "dp"), None),
            P(("tensor", "dp"), None),
            P(("tensor", "dp"), None),
            P(),
            P(),
            P(),
            P(),
            P(),
            P(),
            P(),
            P(),
            P(),
            P(),
            P(),
            P(),
            P(),
            P(),
        ),
        out_specs=(
            P(("dp", "tensor"), None),
            P(),
            P(("dp", "tensor"), None),
            P(("tensor", "dp"), None),
            P(("tensor", "dp"), None),
            P(("tensor", "dp"), None),
            P(("tensor", "dp"), None),
            P(("tensor", "dp"), None),
            P(("tensor", "dp"), None),
            P(),
            P(),
            P(),
            P(),
            P(),
            P(),
            P(),
            P(),
            P(),
            P(),
            P(),
            P(),
            P(),
            P(),
        ),
        check_vma=False,
    )
```

```python
import functools
import math

import jax
import jax.numpy as jnp
from jax import lax
from jax.experimental import pallas as pl
from jax.experimental.pallas import tpu as pltpu
from jax.sharding import PartitionSpec as P

D = 768
HEADS = 12
FF = 3072
SEQ = 1024


epsilon = 1e-12


def norm_rows(summed, gain_vec, shift_vec):
    average = jnp.mean(summed, axis=-1, keepdims=True)
    centered = summed - average
    variance = jnp.mean(centered * centered, axis=-1, keepdims=True)
    return centered * lax.rsqrt(variance + epsilon) * gain_vec + shift_vec


def gelu_exact(values):
    return jax.nn.gelu(values, approximate=False)


def times_plain(left, right):
    return jnp.dot(left, right, preferred_element_type=jnp.float32)


def times_trans(left, right):
    return lax.dot_general(
        left, right, (((1,), (1,)), ((), ())), preferred_element_type=jnp.float32
    )


def trans_times(left, right):
    return lax.dot_general(
        left, right, (((0,), (0,)), ((), ())), preferred_element_type=jnp.float32
    )


def gather_attn(w_query, w_key, w_value, w_out):
    return (
        lax.all_gather(w_query, "dp", axis=0, tiled=True),
        lax.all_gather(w_key, "dp", axis=0, tiled=True),
        lax.all_gather(w_value, "dp", axis=0, tiled=True),
        lax.all_gather(w_out, "dp", axis=0, tiled=True),
    )


def gather_ffn(w_up, w_down):
    return (
        lax.all_gather(w_up, "dp", axis=0, tiled=True),
        lax.all_gather(w_down, "dp", axis=0, tiled=True),
    )


def spread_into(local_vec, full_len, offset):
    return lax.dynamic_update_slice(jnp.zeros((full_len,), jnp.float32), local_vec, (offset,))


def on_device(
    inputs,
    teacher,
    lengths,
    w_query,
    w_key,
    w_value,
    w_out,
    w_up,
    w_down,
    b_query,
    b_value,
    b_out,
    b_up,
    b_down,
    gain_one,
    shift_one,
    gain_two,
    shift_two,
    z_head,
    z_mha,
    z_hidden,
    z_int,
    z_ffn,
):
    rows_own = inputs.shape[0]
    tensor_pos = lax.axis_index("tensor")
    tensor_count = lax.axis_size("tensor")
    group_rows = rows_own * tensor_count
    seq_count = group_rows // SEQ
    head_size = D // HEADS
    local_width = D // tensor_count
    heads_local = local_width // head_size
    units_local = FF // tensor_count
    qblock = min(512, SEQ)
    nblocks = SEQ // qblock
    softmax_scale = 1.0 / math.sqrt(head_size)
    positions = jnp.arange(group_rows, dtype=jnp.int32)
    seq_of_row = positions // SEQ
    picks = seq_of_row[:, None] == jnp.arange(seq_count, dtype=jnp.int32)[None, :]
    row_length = jnp.sum(jnp.where(picks, lengths[None, :], 0), axis=1)
    valid_group = positions % SEQ < row_length
    valid_own = lax.dynamic_slice_in_dim(valid_group, tensor_pos * rows_own, rows_own)
    head_start = tensor_pos * local_width
    unit_start = tensor_pos * units_local
    bias_query = lax.dynamic_slice_in_dim(b_query, head_start, local_width)
    bias_value = lax.dynamic_slice_in_dim(b_value, head_start, local_width)
    gate_heads = lax.dynamic_slice_in_dim(z_head, tensor_pos * heads_local, heads_local)
    bias_up = lax.dynamic_slice_in_dim(b_up, unit_start, units_local)
    gate_units = lax.dynamic_slice_in_dim(z_int, unit_start, units_local)
    wq_full, wk_full, wv_full, wo_full = gather_attn(w_query, w_key, w_value, w_out)
    x_group = lax.all_gather(inputs, "tensor", axis=0, tiled=True)
    query = ((times_trans(x_group, wq_full) + bias_query) * softmax_scale).astype(jnp.bfloat16)
    keys_b = times_trans(x_group, wk_full).astype(jnp.bfloat16)
    values_b = (times_trans(x_group, wv_full) + bias_value).astype(jnp.bfloat16)
    query5 = query.reshape(seq_count, nblocks, qblock, heads_local, head_size)
    keys4 = keys_b.reshape(seq_count, SEQ, heads_local, head_size)
    values4 = values_b.reshape(seq_count, SEQ, heads_local, head_size)
    valid2 = valid_group.reshape(seq_count, SEQ)

    def forward_seq(element):
        query_seq, keys_seq, values_seq, key_valid = element

        def forward_block(query_blk):
            scores = jnp.einsum(
                "qhd,khd->hqk", query_blk, keys_seq, preferred_element_type=jnp.float32
            )
            scores = jnp.where(key_valid[None, None, :], scores, -1e30)
            highest = jnp.max(scores, axis=-1, keepdims=True)
            exponent = jnp.exp(scores - highest)
            denominator = jnp.sum(exponent, axis=-1, keepdims=True)
            attention = (exponent / denominator).astype(jnp.bfloat16)
            context = jnp.einsum(
                "hqk,khd->qhd", attention, values_seq, preferred_element_type=jnp.float32
            )
            return (context, (highest + jnp.log(denominator))[..., 0])

        return lax.map(forward_block, query_seq)

    context_all, logsum_all = lax.map(forward_seq, (query5, keys4, values4, valid2))
    context_f = context_all.reshape(group_rows, heads_local, head_size)
    gated = (
        (context_f * gate_heads[None, :, None])
        .reshape(group_rows, local_width)
        .astype(jnp.bfloat16)
    )
    attn_out = (
        lax.psum_scatter(times_plain(gated, wo_full), "tensor", scatter_dimension=0, tiled=True)
        + b_out
    )
    branch_attn = z_mha * z_hidden
    first_sum = inputs.astype(jnp.float32) + branch_attn * attn_out
    first_norm = norm_rows(first_sum, gain_one, shift_one)
    y_group = lax.all_gather(first_norm.astype(jnp.bfloat16), "tensor", axis=0, tiled=True)
    wu_full, wd_full = gather_ffn(w_up, w_down)
    upper = times_trans(y_group, wu_full) + bias_up
    activated = gelu_exact(upper)
    hidden_b = (activated * gate_units).astype(jnp.bfloat16)
    down = (
        lax.psum_scatter(times_plain(hidden_b, wd_full), "tensor", scatter_dimension=0, tiled=True)
        + b_down
    )
    branch_ffn = z_ffn * z_hidden
    second_sum = first_norm + branch_ffn * down
    output = norm_rows(second_sum, gain_two, shift_two)
    residue = output - teacher.astype(jnp.float32)
    masked = jnp.where(valid_own[:, None], residue, 0.0)
    valid_count, square_sum = lax.psum(
        (jnp.sum(valid_own.astype(jnp.float32)), jnp.sum(masked * masked)), ("dp", "tensor")
    )
    loss_value = square_sum / (D * valid_count)
    tokens_all = group_rows * lax.axis_size("dp")
    grad_out = masked * (2.0 * tokens_all / valid_count)
    ffn_back = gather_ffn(w_up, w_down)
    attn_back = gather_attn(w_query, w_key, w_value, w_out)
    unused, pull_two = jax.vjp(norm_rows, second_sum, gain_two, shift_two)
    grad_second, grad_gain_two, grad_shift_two = pull_two(grad_out)
    grad_down = (grad_second * branch_ffn).astype(jnp.bfloat16)
    grad_z_ffn = jnp.sum(grad_second * z_hidden * down).reshape(1)
    hidden_part = jnp.sum(grad_second * z_ffn * down, axis=0)
    grad_b_down = jnp.sum(grad_down.astype(jnp.float32), axis=0)
    down_group = lax.all_gather(grad_down, "tensor", axis=0, tiled=True)
    grad_w_down = trans_times(hidden_b, down_group)
    grad_hidden = times_trans(down_group, ffn_back[1])
    grad_z_int_local = jnp.sum(grad_hidden * activated, axis=0)
    unused, gelu_pull = jax.vjp(gelu_exact, upper)
    grad_upper = gelu_pull(grad_hidden * gate_units)[0].astype(jnp.bfloat16)
    grad_b_up_local = jnp.sum(grad_upper.astype(jnp.float32), axis=0)
    grad_w_up = trans_times(grad_upper, y_group)
    grad_first_norm = grad_second + lax.psum_scatter(
        times_plain(grad_upper, ffn_back[0]), "tensor", scatter_dimension=0, tiled=True
    )
    unused, pull_one = jax.vjp(norm_rows, first_sum, gain_one, shift_one)
    grad_first, grad_gain_one, grad_shift_one = pull_one(grad_first_norm)
    grad_attn = (grad_first * branch_attn).astype(jnp.bfloat16)
    grad_z_mha = jnp.sum(grad_first * z_hidden * attn_out).reshape(1)
    hidden_part = hidden_part + jnp.sum(grad_first * z_mha * attn_out, axis=0)
    grad_b_out = jnp.sum(grad_attn.astype(jnp.float32), axis=0)
    attn_group = lax.all_gather(grad_attn, "tensor", axis=0, tiled=True)
    grad_w_out = trans_times(gated, attn_group)
    grad_gated = times_trans(attn_group, attn_back[3]).reshape(group_rows, heads_local, head_size)
    grad_z_head_local = jnp.sum(grad_gated * context_f, axis=(0, 2))
    grad_heads = (grad_gated * gate_heads[None, :, None]).astype(jnp.bfloat16)
    grad_heads5 = grad_heads.reshape(seq_count, nblocks, qblock, heads_local, head_size)

    def backward_seq(element):
        query_seq, keys_seq, values_seq, key_valid, grad_seq, logsum_seq = element
        initial = jnp.zeros((SEQ, heads_local, head_size), jnp.float32)

        def backward_block(running, block):
            keys_acc, values_acc = running
            query_blk, grad_blk, logsum_blk = block
            scores = jnp.einsum(
                "qhd,khd->hqk", query_blk, keys_seq, preferred_element_type=jnp.float32
            )
            scores = jnp.where(key_valid[None, None, :], scores, -1e30)
            attention = jnp.exp(scores - logsum_blk[..., None])
            attention_b = attention.astype(jnp.bfloat16)
            grad_attention = jnp.einsum(
                "qhd,khd->hqk", grad_blk, values_seq, preferred_element_type=jnp.float32
            )
            row_dots = jnp.sum(attention * grad_attention, axis=-1, keepdims=True)
            grad_scores = (attention * (grad_attention - row_dots)).astype(jnp.bfloat16)
            grad_query_blk = (
                softmax_scale
                * jnp.einsum(
                    "hqk,khd->qhd", grad_scores, keys_seq, preferred_element_type=jnp.float32
                )
            ).astype(jnp.bfloat16)
            keys_acc = keys_acc + jnp.einsum(
                "hqk,qhd->khd", grad_scores, query_blk, preferred_element_type=jnp.float32
            )
            values_acc = values_acc + jnp.einsum(
                "hqk,qhd->khd", attention_b, grad_blk, preferred_element_type=jnp.float32
            )
            return ((keys_acc, values_acc), grad_query_blk)

        (keys_acc, values_acc), grad_query_seq = lax.scan(
            backward_block, (initial, initial), (query_seq, grad_seq, logsum_seq)
        )
        return (grad_query_seq, keys_acc.astype(jnp.bfloat16), values_acc.astype(jnp.bfloat16))

    grad_query_all, grad_keys_all, grad_values_all = lax.map(
        backward_seq, (query5, keys4, values4, valid2, grad_heads5, logsum_all)
    )
    grad_query = grad_query_all.reshape(group_rows, local_width)
    grad_keys = grad_keys_all.reshape(group_rows, local_width)
    grad_values = grad_values_all.reshape(group_rows, local_width)
    grad_w_query = trans_times(grad_query, x_group)
    grad_w_key = trans_times(grad_keys, x_group)
    grad_w_value = trans_times(grad_values, x_group)
    grad_b_query_local = jnp.sum(grad_query.astype(jnp.float32), axis=0)
    grad_b_value_local = jnp.sum(grad_values.astype(jnp.float32), axis=0)
    part_query = times_plain(grad_query, attn_back[0])
    part_keys = times_plain(grad_keys, attn_back[1])
    part_values = times_plain(grad_values, attn_back[2])
    grad_inputs = grad_first + lax.psum_scatter(
        (part_query + part_keys + part_values).astype(jnp.bfloat16),
        "tensor",
        scatter_dimension=0,
        tiled=True,
    ).astype(jnp.float32)
    shard_wq, shard_wk, shard_wv, shard_wo, shard_wu, shard_wd = (
        lax.psum_scatter(grad_w_query, "dp", scatter_dimension=0, tiled=True),
        lax.psum_scatter(grad_w_key, "dp", scatter_dimension=0, tiled=True),
        lax.psum_scatter(grad_w_value, "dp", scatter_dimension=0, tiled=True),
        lax.psum_scatter(grad_w_out, "dp", scatter_dimension=0, tiled=True),
        lax.psum_scatter(grad_w_up, "dp", scatter_dimension=0, tiled=True),
        lax.psum_scatter(grad_w_down, "dp", scatter_dimension=0, tiled=True),
    )
    small_sums = lax.psum(
        (
            spread_into(grad_b_query_local, D, head_start),
            spread_into(grad_b_value_local, D, head_start),
            grad_b_out,
            spread_into(grad_b_up_local, FF, unit_start),
            grad_b_down,
            grad_gain_one,
            grad_shift_one,
            grad_gain_two,
            grad_shift_two,
            spread_into(grad_z_head_local, HEADS, tensor_pos * heads_local),
            grad_z_mha,
            hidden_part,
            spread_into(grad_z_int_local, FF, unit_start),
            grad_z_ffn,
        ),
        ("dp", "tensor"),
    )
    return (
        output,
        loss_value.reshape(1),
        grad_inputs,
        shard_wq,
        shard_wk,
        shard_wv,
        shard_wo,
        shard_wu,
        shard_wd,
        small_sums[0],
        small_sums[1],
        small_sums[2],
        small_sums[3],
        small_sums[4],
        small_sums[5],
        small_sums[6],
        small_sums[7],
        small_sums[8],
        small_sums[9],
        small_sums[10],
        small_sums[11],
        small_sums[12],
        small_sums[13],
    )


MESH = pl.DeviceIdType.MESH
F32 = jnp.float32
BF16 = jnp.bfloat16
ROWS = 512
SCALE = 0.125
BQ, BV, BO, BD, G1, S1, G2, S2, ZH, BU, ZI, SC = 0, 1, 2, 3, 4, 5, 6, 7, 8, 9, 13, 17
ROOT_HALF = math.sqrt(0.5)
DENSITY = 1.0 / math.sqrt(2.0 * math.pi)


def place():
    dp = lax.axis_index("dp")
    return dp // 4, (dp // 2) % 2, dp % 2, lax.axis_index("tensor")


def device(z, x, c, y):
    return ((z * 2 + x) * 2 + c, y)


def shard_of(z, x, c, y):
    return y * 16 + z * 4 + x * 2 + c


def remote(src, dst, send_sem, recv_sem, to):
    return pltpu.make_async_remote_copy(
        src_ref=src,
        dst_ref=dst,
        send_sem=send_sem,
        recv_sem=recv_sem,
        device_id=to,
        device_id_type=MESH,
    )


def greet(partners):
    barrier = pltpu.get_barrier_semaphore()
    for partner in partners:
        pl.semaphore_signal(barrier, inc=1, device_id=partner, device_id_type=MESH)
    pl.semaphore_wait(barrier, len(partners))


def peers(axis):
    return (1, 2, 3) if axis == "z" else (1,)


def offsets(order):
    found = [()]
    for axis in order:
        found = [o + (v,) for o in found for v in (0,) + peers(axis)]
    return found


class Around:
    def __init__(self):
        self.z, self.x, self.c, self.y = place()
        self.sibling = device(self.z, self.x, 1 - self.c, self.y)
        self.across = device(self.z, self.x, 1 - self.c, 1 - self.y)
        self.all = [self.sibling, self.across]
        self.all += [self.peer("z", v) for v in (1, 2, 3)] + [self.peer("x", 1), self.peer("y", 1)]

    def at(self, order, offset, c):
        z, x, y = self.z, self.x, self.y
        for axis, v in zip(order, offset):
            if v == 0:
                continue
            if axis == "z":
                z = z ^ v
            elif axis == "x":
                x = 1 - x
            elif axis == "y":
                y = 1 - y
            elif axis == "f":
                x, y = x ^ c, y ^ (1 - c)
            else:
                x, y = x ^ (1 - c), y ^ c
        return z, x, y

    def peer(self, axis, v):
        z, x, y = self.at(axis, (v,), self.c)
        return device(z, x, self.c, y)

    def shard(self, order, offset, c):
        z, x, y = self.at(order, offset, c)
        return shard_of(z, x, c, y)


class Gather:
    def __init__(self, d, order, own, full_at, send_sems, recv_sems):
        self.d, self.order, self.own, self.full_at = d, order, own, full_at
        self.send_sems, self.recv_sems = send_sems, recv_sems
        self.slots = {o: i for i, o in enumerate(offsets(order))}
        self.sent = 0
        rest = [o for o in self.slots if any(o)]
        rest.sort(key=lambda o: (sum(v > 0 for v in o), self.last(o), o))
        self.events = [functools.partial(self.pass_on, o) for o in rest]

    def last(self, offset):
        return max(i for i, v in enumerate(offset) if v)

    def send(self, src, shard, slot, to):
        sem = self.send_sems.at[self.sent]
        self.sent += 1
        remote(src, self.full_at(shard), sem, self.recv_sems.at[slot], to).start()

    def spread(self, src, offset, start):
        shard = self.d.shard(self.order, offset, self.d.c)
        for i in reversed(range(start, len(self.order))):
            for v in peers(self.order[i]):
                there = offset[:i] + (v,) + offset[i + 1 :]
                self.send(src, shard, self.slots[there], self.d.peer(self.order[i], v))
        self.send(src, shard, 16 + self.slots[offset], self.d.sibling)

    def begin(self):
        self.spread(self.own, (0,) * len(self.order), 0)

    def wait(self, shard, slot):
        ref = self.full_at(shard)
        remote(
            ref, ref, self.send_sems.at[0], self.recv_sems.at[slot], self.d.sibling
        ).wait_recv()

    def pass_on(self, offset):
        shard = self.d.shard(self.order, offset, self.d.c)
        self.wait(shard, self.slots[offset])
        self.spread(self.full_at(shard), offset, self.last(offset) + 1)

    def arrive(self):
        for o, slot in self.slots.items():
            self.wait(self.d.shard(self.order, o, 1 - self.d.c), 16 + slot)

    def finish(self):
        for i in range(self.sent):
            remote(
                self.own, self.own, self.send_sems.at[i], self.recv_sems.at[0], self.d.sibling
            ).wait_send()


GATHER_SEMS = 31


def sum_refs(target, sources, step):
    if len(target.shape) == 3:
        for i in range(target.shape[0]):
            sum_refs(target.at[i], [s.at[i] for s in sources], step)
        return

    def body(i, carry):
        span = pl.ds(pl.multiple_of(i * step, step), step)
        total = sources[0][span, :].astype(F32)
        for source in sources[1:]:
            total = total + source[span, :].astype(F32)
        target[span, :] = total.astype(target.dtype)
        return carry

    lax.fori_loop(0, target.shape[0] // step, body, 0)


class Scatter:
    def __init__(self, d, order, part_at, own, landed, send_sems, recv_sems, total, step):
        self.d, self.order, self.part_at, self.own, self.landed = d, order, part_at, own, landed
        self.send_sems, self.recv_sems, self.total, self.step = send_sems, recv_sems, total, step
        self.slots = {o: i for i, o in enumerate(offsets(order))}
        self.lands = {}
        for i, axis in enumerate(order):
            for v in peers(axis):
                for rest in offsets(order[i + 1 :]):
                    self.lands[(i, v, rest)] = len(self.lands)
        self.sent = 0
        self.todo = sorted(
            (o for o in self.slots if any(o)),
            key=lambda o: (self.first(o), -sum(v > 0 for v in o), o),
        )
        self.events = [functools.partial(self.pass_on, o) for o in self.todo]

    def first(self, offset):
        return min(i for i, v in enumerate(offset) if v)

    def send(self, src, dst, slot, to):
        sem = self.send_sems.at[self.sent]
        self.sent += 1
        remote(src, dst, sem, self.recv_sems.at[slot], to).start()

    def begin(self):
        for o in self.todo + [(0,) * len(self.order)]:
            slot = self.slots[o]
            shard = self.d.shard(self.order, o, 1 - self.d.c)
            self.send(self.part_at(shard), self.own.at[slot], slot, self.d.sibling)

    def wait(self, ref, slot):
        remote(
            ref, ref, self.send_sems.at[0], self.recv_sems.at[slot], self.d.sibling
        ).wait_recv()

    def gathered(self, offset, until):
        slot = self.slots[offset]
        self.wait(self.own.at[slot], slot)
        found = [self.own.at[slot], self.part_at(self.d.shard(self.order, offset, self.d.c))]
        for i in range(until):
            for v in peers(self.order[i]):
                land = self.lands[(i, v, offset[i + 1 :])]
                self.wait(self.landed.at[land], 16 + land)
                found.append(self.landed.at[land])
        return found

    def pass_on(self, offset):
        i = self.first(offset)
        slot = self.slots[offset]
        sum_refs(self.own.at[slot], self.gathered(offset, i), self.step)
        land = self.lands[(i, offset[i], offset[i + 1 :])]
        self.send(
            self.own.at[slot],
            self.landed.at[land],
            16 + land,
            self.d.peer(self.order[i], offset[i]),
        )

    def collect(self):
        sum_refs(self.total, self.gathered((0,) * len(self.order), len(self.order)), self.step)

    def finish(self):
        ref = self.own.at[0]
        for i in range(self.sent):
            remote(
                ref, ref, self.send_sems.at[i], self.recv_sems.at[0], self.d.sibling
            ).wait_send()


SCATTER_SEMS = 31


def any_spec():
    return pl.BlockSpec(memory_space=pl.ANY)


def vmem_spec():
    return pl.BlockSpec(memory_space=pltpu.VMEM)


def smem_spec():
    return pl.BlockSpec(memory_space=pltpu.SMEM)


def shaped(shape, dtype):
    return jax.ShapeDtypeStruct(shape, dtype)


def vmem(shape, dtype):
    return pltpu.VMEM(shape, dtype)


def dma(*shape):
    return pltpu.SemaphoreType.DMA(shape)


def run_at(p, chunks):
    for i, chunk in enumerate(chunks):
        if not chunk:
            continue

        @pl.when(p == i)
        def _(chunk=chunk):
            for call in chunk:
                call()


def shared_out(calls, count):
    per = -(-len(calls) // count)
    return [calls[i * per : (i + 1) * per] for i in range(count)]


def stack_head(rows, half):
    blank = jnp.zeros_like(rows)
    return jnp.concatenate([rows, blank] if half == 0 else [blank, rows], axis=0)


def key_mask(mask, length):
    row = lax.broadcasted_iota(jnp.int32, (2 * ROWS // 8, 8, 128), 0) * 8
    row = row + lax.broadcasted_iota(jnp.int32, (2 * ROWS // 8, 8, 128), 1)
    mask[...] = jnp.where(row.astype(F32) < length[None], 0.0, -1e30).reshape(2 * ROWS, 128)


def front_kernel(
    lengths, z_head, x_in, wq, wk, wv, wo, wu, bq, bv,
    x, marks, w4, wu_full, q, qt, k, kt, v, ot, ctx, lse,
    own4, mark, w3, vt, mask,
    s4, r4, su, ru, sm, rm, swap_s, swap_r, pair_s, pair_r, load,
):
    d = Around()
    z, c, y = d.z, d.c, d.y
    for i, shard in enumerate((wq, wk, wv, wo)):
        own4[i] = shard[...]
    mark[...] = jnp.full((8, 128), lengths[0], jnp.int32).astype(F32)
    greet(d.all)
    swap = remote(x_in, x, swap_s.at[0], swap_r.at[0], d.across)

    @pl.when(c != y)
    def _():
        swap.start()

    def rows24(shard):
        return w4.at[:, pl.ds(pl.multiple_of(shard * 24, 24), 24), :]

    def rows96(shard):
        return wu_full.at[pl.ds(pl.multiple_of(shard * 96, 96), 96), :]

    first = Gather(d, "zyx", own4, rows24, s4, r4)
    small = Gather(d, "zyx", mark, lambda shard: marks.at[shard], sm, rm)
    ups = Gather(d, "zfs", wu, rows96, su, ru)
    me = shard_of(z, d.x, c, y)
    keep = [
        pltpu.make_async_copy(own4, rows24(me), load.at[0]),
        pltpu.make_async_copy(wu, rows96(me), load.at[1]),
    ]
    first.begin()
    small.begin()
    for copy in keep:
        copy.start()
    marks[me] = mark[...]

    @pl.when(c == y)
    def _():
        x[...] = x_in[...]

    for one, two in zip(first.events, small.events):
        one()
        two()
    ups.begin()
    keep[0].wait()
    first.arrive()
    load3 = [pltpu.make_async_copy(w4.at[i], w3.at[i], load.at[2 + i]) for i in range(3)]
    for copy in load3:
        copy.start()

    @pl.when(c != y)
    def _():
        swap.wait()

    xv = x[...]

    def share(i, buf):
        copy = remote(buf.at[c], buf.at[c], pair_s.at[i], pair_r.at[i], d.sibling)
        copy.start()
        return copy

    load3[1].wait()
    keys = times_trans(xv, w3[1])
    k[c] = keys.astype(BF16)
    copies = [share(0, k)]
    kt[c] = keys.T.astype(BF16)
    copies.append(share(1, kt))
    load3[2].wait()
    values = times_trans(xv, w3[2]) + bv[...].reshape(1, D)
    v[c] = values.astype(BF16)
    copies.append(share(2, v))
    vt[c] = values.T.astype(BF16)
    copies.append(share(3, vt))
    load3[0].wait()
    query = (times_trans(xv, w3[0]) + bq[...].reshape(1, D)) * SCALE
    q[...] = query.astype(BF16)
    qt[...] = query.T.astype(BF16)
    small.arrive()
    key_mask(mask, marks[z * 4 + d.x * 2 + y])
    for i, buf in enumerate((k, kt, v, vt)):
        remote(
            buf.at[1 - c], buf.at[1 - c], pair_s.at[i], pair_r.at[i], d.sibling
        ).wait_recv()
    chunks = shared_out(ups.events, HEADS // 2)

    def pair_body(p, carry):
        run_at(p, chunks)
        lanes = pl.ds(pl.multiple_of(p * 128, 128), 128)
        kp = k[:, :, lanes].reshape(2 * ROWS, 128)
        off = jnp.concatenate([mask[...]] * 4, axis=1)
        for half in (0, 1):
            h = p * 2 + half
            span = pl.ds(pl.multiple_of(h * 64, 64), 64)
            s = times_plain(kp, stack_head(qt[span, :], half)) + off
            top = jnp.max(s, axis=0, keepdims=True)
            e = jnp.exp(s - top)
            den = jnp.sum(e, axis=0, keepdims=True)
            probs = (e * (1.0 / den)).astype(BF16)
            ot[span, :] = times_plain(vt[0, span, :], probs[:ROWS]) + times_plain(
                vt[1, span, :], probs[ROWS:]
            )
            lse[pl.ds(h, 1), :] = top + jnp.log(den)
        return carry

    lax.fori_loop(0, HEADS // 2, pair_body, 0)
    for h in range(HEADS):
        span = slice(h * 64, h * 64 + 64)
        ctx[:, span] = (ot[span, :] * z_head[h]).T.astype(BF16)
    keep[1].wait()
    ups.arrive()
    for copy in copies:
        copy.wait_send()
    for gather in (first, small, ups):
        gather.finish()


def front(lengths, z_head, x, wq, wk, wv, wo, wu, bq, bv):
    return pl.pallas_call(
        front_kernel,
        out_shape=(
            shaped((ROWS, D), BF16),
            shaped((32, 8, 128), F32),
            shaped((4, D, D), BF16),
            shaped((FF, D), BF16),
            shaped((ROWS, D), BF16),
            shaped((D, ROWS), BF16),
            shaped((2, ROWS, D), BF16),
            shaped((2, D, ROWS), BF16),
            shaped((2, ROWS, D), BF16),
            shaped((D, ROWS), F32),
            shaped((ROWS, D), BF16),
            shaped((HEADS, ROWS), F32),
        ),
        in_specs=[smem_spec()] * 2 + [vmem_spec()] * 8,
        out_specs=(vmem_spec(),) * 2 + (any_spec(),) * 2 + (vmem_spec(),) * 8,
        scratch_shapes=[
            vmem((4, 24, D), BF16),
            vmem((8, 128), F32),
            vmem((3, D, D), BF16),
            vmem((2, D, ROWS), BF16),
            vmem((2 * ROWS, 128), F32),
            dma(GATHER_SEMS), dma(32), dma(GATHER_SEMS), dma(32), dma(GATHER_SEMS), dma(32),
            dma(1), dma(1), dma(4), dma(4), dma(5),
        ],
        compiler_params=pltpu.CompilerParams(
            collective_id=1, has_side_effects=True, vmem_limit_bytes=60 << 20
        ),
        name="front",
    )(lengths, z_head, x, wq, wk, wv, wo, wu, bq, bv)


def rows_loop(body, step=128):
    def run(i, carry):
        body(i * step, pl.ds(pl.multiple_of(i * step, step), step))
        return carry

    lax.fori_loop(0, ROWS // step, run, 0)


def col_sum(values):
    return jnp.sum(values, axis=0, keepdims=True)


def row_mean(values):
    return jnp.sum(values, axis=1, keepdims=True) * (1.0 / D)


def mid_kernel(
    zm, zf, z_head,
    marks, x, t_in, ctx, ot, wo, wu, wd_own, bo, bu, bd, g1, s1, g2, s2, zh, zi,
    out, dwu, dwo, gfirst, g, gt, vec, wd_sum,
    t, wd, dwd, attn, fn, xh1, r1, low, up, cdf, hid, gdown, acc, own_d, land_d,
    sd, rd, ssd, rsd, swap_s, swap_r, load,
):
    d = Around()
    z, c, y = d.z, d.c, d.y
    greet(d.all)
    gather = Gather(d, "zfs", wd_own, lambda shard: wd.at[shard], sd, rd)
    scatter = Scatter(
        d, "sfz", lambda shard: dwd.at[shard], own_d, land_d, ssd, rsd, wd_sum, 48
    )
    gather.begin()
    wd[shard_of(z, d.x, c, y)] = wd_own[...]
    swap = remote(t_in, t, swap_s.at[0], swap_r.at[0], d.across)

    @pl.when(c != y)
    def _():
        swap.start()

    @pl.when(c == y)
    def _():
        t[...] = t_in[...]

    vec[...] = jnp.zeros_like(vec)
    lane = lax.broadcasted_iota(jnp.int32, (1, D), 1)
    row = lambda ref: ref[...].reshape(1, -1)

    def add(at, value):
        vec[at : at + 1, :] += value

    def add_scalar(at, value):
        vec[SC : SC + 1, :] += jnp.where(lane == at, value, 0.0)

    attn[...] = times_plain(ctx[...], wo[...]) + row(bo)
    ba = zm[0] * row(zh)
    bf = zf[0] * row(zh)

    def first(at, span):
        h = x[span, :].astype(F32) + ba * attn[span, :]
        cen = h - row_mean(h)
        r = lax.rsqrt(row_mean(cen * cen) + epsilon)
        xh = cen * r
        xh1[span, :] = xh
        r1[span, :] = jnp.broadcast_to(r, (128, 128))
        f = xh * row(g1) + row(s1)
        fn[span, :] = f
        low[span, :] = f.astype(BF16)

    rows_loop(first)
    chunks = shared_out(gather.events, FF // D)

    def unit_up(j, carry):
        run_at(j, chunks)
        units = pl.ds(pl.multiple_of(j * D, D), D)
        u = times_trans(low[...], wu[units, :]) + bu[pl.ds(j, 1), :]
        up[:, units] = u
        cd = 0.5 * (1.0 + lax.erf(u * ROOT_HALF))
        cdf[:, units] = cd
        hid[:, units] = (u * cd * zi[pl.ds(j, 1), :]).astype(BF16)
        return carry

    lax.fori_loop(0, FF // D, unit_up, 0)
    gather.arrive()
    acc[...] = jnp.zeros_like(acc)

    def shards(ref, j):
        return ref[pl.ds(pl.multiple_of(j * 8, 8), 8)].reshape(D, D)

    def unit_down(j, carry):
        units = pl.ds(pl.multiple_of(j * D, D), D)
        acc[...] += times_plain(hid[:, units], shards(wd, j))
        return carry

    lax.fori_loop(0, FF // D, unit_down, 0)

    @pl.when(c != y)
    def _():
        swap.wait()

    total = marks[0]
    for i in range(1, 16):
        total = total + marks[i]
    scale = (2.0 * 32 * ROWS) / total[0:1, 0:1]
    length = marks[z * 4 + d.x * 2 + y][0:1, 0:1]

    def second(at, span):
        down = acc[span, :] + row(bd)
        h = fn[span, :] + bf * down
        cen = h - row_mean(h)
        r = lax.rsqrt(row_mean(cen * cen) + epsilon)
        xh = cen * r
        o = xh * row(g2) + row(s2)
        out[span, :] = o
        pos = lax.broadcasted_iota(jnp.int32, (128, D), 0) + (c * ROWS + at)
        res = jnp.where(pos.astype(F32) < length, o - t[span, :].astype(F32), 0.0)
        add_scalar(14, jnp.sum(res * res))
        go = res * scale
        add(G2, col_sum(go * xh))
        add(S2, col_sum(go))
        e = go * row(g2)
        gs = r * (e - row_mean(e) - xh * row_mean(e * xh))
        acc[span, :] = gs
        gd = (gs * bf).astype(BF16)
        gdown[span, :] = gd
        add(BD, col_sum(gd.astype(F32)))
        gsd = gs * down
        add_scalar(13, jnp.sum(gsd * row(zh)))
        add(ZH, col_sum(gsd * zf[0]))

    rows_loop(second)

    def down_back(j, carry):
        units = pl.ds(pl.multiple_of(j * D, D), D)
        dw = trans_times(hid[:, units], gdown[...]).astype(BF16)
        dwd[pl.ds(pl.multiple_of(j * 8, 8), 8)] = dw.reshape(8, 96, D)
        return carry

    lax.fori_loop(0, FF // D, down_back, 0)
    scatter.begin()
    chunks_back = shared_out(scatter.events, FF // D)

    def unit_back(j, carry):
        units = pl.ds(pl.multiple_of(j * D, D), D)
        gh = times_trans(gdown[...], shards(wd, j))
        u = up[:, units]
        cd = cdf[:, units]
        vec[pl.ds(ZI + j, 1), :] = col_sum(gh * (u * cd))
        gu = gh * zi[pl.ds(j, 1), :] * (cd + u * (DENSITY * jnp.exp(-0.5 * u * u)))
        gu = gu.astype(BF16)
        vec[pl.ds(BU + j, 1), :] = col_sum(gu.astype(F32))
        acc[...] += times_plain(gu, wu[units, :])
        dwu[units, :] = trans_times(gu, low[...]).astype(BF16)
        run_at(j, chunks_back)
        return carry

    lax.fori_loop(0, FF // D, unit_back, 0)

    def third(at, span):
        gf = acc[span, :]
        xh = xh1[span, :]
        add(G1, col_sum(gf * xh))
        add(S1, col_sum(gf))
        e = gf * row(g1)
        gr = r1[span, 0:1] * (e - row_mean(e) - xh * row_mean(e * xh))
        gfirst[span, :] = gr
        ga = (gr * ba).astype(BF16)
        low[span, :] = ga
        add(BO, col_sum(ga.astype(F32)))
        gra = gr * attn[span, :]
        add_scalar(12, jnp.sum(gra * row(zh)))
        add(ZH, col_sum(gra * zm[0]))

    rows_loop(third)
    dwo[...] = trans_times(ctx[...], low[...]).astype(BF16)
    gct = times_trans(wo[...], low[...])
    for h in range(HEADS):
        span = slice(h * 64, h * 64 + 64)
        block = gct[span, :]
        add_scalar(h, jnp.sum(block * ot[span, :]))
        gb = block * z_head[h]
        gt[span, :] = gb.astype(BF16)
        g[:, span] = gb.T.astype(BF16)
    scatter.collect()
    gather.finish()
    scatter.finish()


def mid(zm, zf, z_head, *arrays):
    return pl.pallas_call(
        mid_kernel,
        out_shape=(
            shaped((ROWS, D), F32),
            shaped((FF, D), BF16),
            shaped((D, D), BF16),
            shaped((ROWS, D), F32),
            shaped((ROWS, D), BF16),
            shaped((D, ROWS), BF16),
            shaped((24, D), F32),
            shaped((96, D), F32),
        ),
        in_specs=[smem_spec()] * 3 + [vmem_spec()] * len(arrays),
        out_specs=(vmem_spec(),) * 8,
        scratch_shapes=[
            vmem((ROWS, D), BF16),
            vmem((32, 96, D), BF16),
            vmem((32, 96, D), BF16),
            vmem((ROWS, D), F32),
            vmem((ROWS, D), F32),
            vmem((ROWS, D), F32),
            vmem((ROWS, 128), F32),
            vmem((ROWS, D), BF16),
            vmem((ROWS, FF), F32),
            vmem((ROWS, FF), F32),
            vmem((ROWS, FF), BF16),
            vmem((ROWS, D), BF16),
            vmem((ROWS, D), F32),
            vmem((16, 96, D), BF16),
            vmem((15, 96, D), BF16),
            dma(GATHER_SEMS), dma(32), dma(SCATTER_SEMS), dma(31), dma(1), dma(1), dma(1),
        ],
        compiler_params=pltpu.CompilerParams(
            collective_id=2, has_side_effects=True, vmem_limit_bytes=63 << 20
        ),
        name="mid",
    )(zm, zf, z_head, *arrays)


def back_kernel(
    marks, x, w4, q, qt, k, kt, v, g, gt, ot, lse, gfirst, vec_in, dwu, dwo, out_in,
    gin, sum_u, sum_o, sum_q, out_swap, gin_swap, vec,
    dqt, dkp, dvp, mask, rk, rv, w3, dw, dwo_s, own_u, land_u, own_o, land_o, own_q, land_q, va, vb, gin_low,
    send, recv, su, ru, so, ro, sq, rq, vec_s, vec_r, swap_s, swap_r, load,
):
    d = Around()
    z, c, y = d.z, d.c, d.y
    greet(d.all)
    swap_o = remote(out_in, out_swap, swap_s.at[0], swap_r.at[0], d.across)

    @pl.when(c != y)
    def _():
        swap_o.start()

    load3 = [pltpu.make_async_copy(w4.at[i], w3.at[i], load.at[i]) for i in range(3)]
    for copy in load3:
        copy.start()
    rows96 = lambda s: dwu.at[pl.ds(pl.multiple_of(s * 96, 96), 96), :]
    ups = Scatter(d, "sfz", rows96, own_u, land_u, su, ru, sum_u, 48)
    outs = Scatter(d, "sfz", lambda s: dwo_s.at[s], own_o, land_o, so, ro, sum_o, 24)
    qkv = Scatter(d, "xyz", lambda s: dw.at[:, s], own_q, land_q, sq, rq, sum_q, 24)
    ups.begin()
    dwo_s[...] = dwo[...].astype(F32).reshape(32, 24, D).astype(BF16)
    outs.begin()
    key_mask(mask, marks[z * 4 + d.x * 2 + y])
    lane = lax.broadcasted_iota(jnp.int32, (ROWS, 128), 1)
    chunks = shared_out([e for pair in zip(ups.events, outs.events) for e in pair], HEADS // 2)

    def pair_body(p, carry):
        lanes = pl.ds(pl.multiple_of(p * 128, 128), 128)
        kp = k[:, :, lanes].reshape(2 * ROWS, 128)
        vp = v[:, :, lanes].reshape(2 * ROWS, 128)
        qp = q[:, lanes]
        gp = g[:, lanes]
        off = jnp.concatenate([mask[...]] * 4, axis=1)
        zero = jnp.zeros_like(qp)
        dka = []
        dva = []
        for half in (0, 1):
            h = p * 2 + half
            span = pl.ds(pl.multiple_of(h * 64, 64), 64)
            mine = (lane >= 64) if half else (lane < 64)
            s = times_plain(kp, stack_head(qt[span, :], half)) + off
            probs = jnp.exp(s - lse[pl.ds(h, 1), :])
            gth = gt[span, :]
            gp_t = times_plain(vp, stack_head(gth, half))
            dots = col_sum(gth.astype(F32) * ot[span, :])
            ds = (probs * (gp_t - dots)).astype(BF16)
            dka.append(times_plain(ds, jnp.where(mine, qp, zero)))
            dva.append(times_plain(probs.astype(BF16), jnp.where(mine, gp, zero)))
            dq = times_plain(kt[0, span, :], ds[:ROWS]) + times_plain(kt[1, span, :], ds[ROWS:])
            dqt[span, :] = (dq * SCALE).astype(BF16)
        dkp[:, :, lanes] = (dka[0] + dka[1]).reshape(2, ROWS, 128)
        dvp[:, :, lanes] = (dva[0] + dva[1]).reshape(2, ROWS, 128)
        run_at(p, chunks)
        return carry

    lax.fori_loop(0, HEADS // 2, pair_body, 0)
    copies = [
        remote(dkp.at[1 - c], rk, send.at[0], recv.at[0], d.sibling),
        remote(dvp.at[1 - c], rv, send.at[1], recv.at[1], d.sibling),
    ]
    for copy in copies:
        copy.start()

    def keep(i, value):
        dw[i] = value.reshape(32, 24, D).astype(BF16)

    keep(0, times_plain(dqt[...], x[...]))
    dq = dqt[...].astype(F32).T
    va[0] = vec_in[...]
    va[0, BQ : BQ + 1, :] = col_sum(dq)
    for copy in copies:
        copy.wait()
    dk = (dkp[c] + rk[...]).astype(BF16)
    dv = (dvp[c] + rv[...]).astype(BF16)
    va[0, BV : BV + 1, :] = col_sum(dv.astype(F32))
    keep(1, trans_times(dk, x[...]))
    keep(2, trans_times(dv, x[...]))
    qkv.begin()
    sums = [
        remote(va.at[i], vb.at[i], vec_s.at[i], vec_r.at[i], to)
        for i, to in enumerate(
            (d.sibling, d.peer("x", 1), d.peer("y", 1), d.peer("z", 1), d.peer("z", 2))
        )
    ]
    sums[0].start()
    for event in qkv.events[:2]:
        event()
    for copy in load3:
        copy.wait()
    total = gfirst[...] + times_plain(dq.astype(BF16), w3[0])
    total = total + times_plain(dk, w3[1]) + times_plain(dv, w3[2])
    gin[...] = total
    gin_low[...] = total.astype(BF16)
    swap_g = remote(gin_low, gin_swap, swap_s.at[1], swap_r.at[1], d.across)

    @pl.when(c != y)
    def _():
        swap_g.start()

    def add_up(i):
        sums[i].wait_recv()
        if i == 4:
            vec[...] = va[i] + vb[i]
        else:
            va[i + 1] = va[i] + vb[i]
            sums[i + 1].start()

    add_up(0)
    for i, event in enumerate(qkv.events[2:]):
        event()
        if i in (4, 7, 10):
            add_up({4: 1, 7: 2, 10: 3}[i])
    add_up(4)
    ups.collect()
    outs.collect()
    qkv.collect()
    for copy in sums:
        copy.wait_send()
    for scatter in (ups, outs, qkv):
        scatter.finish()

    @pl.when(c != y)
    def _():
        swap_o.wait()
        swap_g.wait()


def back(*arrays):
    return pl.pallas_call(
        back_kernel,
        out_shape=(
            shaped((ROWS, D), F32),
            shaped((96, D), F32),
            shaped((24, D), F32),
            shaped((3, 24, D), F32),
            shaped((ROWS, D), BF16),
            shaped((ROWS, D), BF16),
            shaped((24, D), F32),
        ),
        in_specs=[vmem_spec()] * 2 + [any_spec()] + [vmem_spec()] * 13 + [any_spec()],
        out_specs=(vmem_spec(),) * 4 + (any_spec(),) * 2 + (vmem_spec(),),
        scratch_shapes=[
            vmem((D, ROWS), BF16),
            vmem((2, ROWS, D), F32),
            vmem((2, ROWS, D), F32),
            vmem((2 * ROWS, 128), F32),
            vmem((ROWS, D), F32),
            vmem((ROWS, D), F32),
            vmem((3, D, D), BF16),
            vmem((3, 32, 24, D), BF16),
            vmem((32, 24, D), BF16),
            vmem((16, 96, D), BF16), vmem((15, 96, D), BF16),
            vmem((16, 24, D), BF16), vmem((15, 24, D), BF16),
            vmem((16, 3, 24, D), BF16), vmem((15, 3, 24, D), BF16),
            vmem((5, 24, D), F32), vmem((5, 24, D), F32),
            vmem((ROWS, D), BF16),
            dma(2), dma(2),
            dma(SCATTER_SEMS), dma(31), dma(SCATTER_SEMS), dma(31), dma(SCATTER_SEMS), dma(31),
            dma(5), dma(5), dma(2), dma(2), dma(3),
        ],
        compiler_params=pltpu.CompilerParams(
            collective_id=3, has_side_effects=True, vmem_limit_bytes=63 << 20
        ),
        name="back",
    )(*arrays)


def by_chip(
    inputs,
    teacher,
    lengths,
    w_query,
    w_key,
    w_value,
    w_out,
    w_up,
    w_down,
    b_query,
    b_value,
    b_out,
    b_up,
    b_down,
    gain_one,
    shift_one,
    gain_two,
    shift_two,
    z_head,
    z_mha,
    z_hidden,
    z_int,
    z_ffn,
):
    z, x, core, y = place()
    source, marks, w4, wu, q, qt, k, kt, v, ot, ctx, lse = front(
        lengths, z_head, inputs, w_query, w_key, w_value, w_out, w_up, b_query, b_value
    )
    output, dwu, dwo, gfirst, g, gt, vec, sum_d = mid(
        z_mha, z_ffn, z_head,
        marks, source, teacher, ctx, ot, w4[3], wu, w_down, b_out, b_up.reshape(4, D), b_down,
        gain_one, shift_one, gain_two, shift_two, z_hidden, z_int.reshape(4, D),
    )
    grad_inputs, sum_u, sum_o, sum_q, out_swap, grad_swap, sums = back(
        marks, source, w4, q, qt, k, kt, v, g, gt, ot, lse, gfirst, vec, dwu, dwo,
        output.astype(BF16),
    )
    home = core == y
    layer_out = jnp.where(home, output, out_swap.astype(F32))
    grad_home = jnp.where(home, grad_inputs, grad_swap.astype(F32))
    valid_count = jnp.sum(marks[:16, 0, 0]).reshape(1)
    return (
        layer_out,
        sums[SC, 14:15] / (D * valid_count),
        grad_home,
        sum_q[0],
        sum_q[1],
        sum_q[2],
        sum_o,
        sum_u,
        sum_d,
        sums[BQ],
        sums[BV],
        sums[BO],
        sums[BU : BU + 4].reshape(-1),
        sums[BD],
        sums[G1],
        sums[S1],
        sums[G2],
        sums[S2],
        sums[SC, 0:12],
        sums[SC, 12:13],
        sums[ZH],
        sums[ZI : ZI + 4].reshape(-1),
        sums[SC, 13:14],
    )


def solution(mesh):
    sizes = (mesh.shape["dp"], mesh.shape["tensor"])
    return jax.shard_map(
        by_chip if sizes == (16, 2) else on_device,
        mesh=mesh,
        in_specs=(
            P(("dp", "tensor"), None),
            P(("dp", "tensor"), None),
            P("dp"),
            P(("tensor", "dp"), None),
            P(("tensor", "dp"), None),
            P(("tensor", "dp"), None),
            P(("tensor", "dp"), None),
            P(("tensor", "dp"), None),
            P(("tensor", "dp"), None),
            P(),
            P(),
            P(),
            P(),
            P(),
            P(),
            P(),
            P(),
            P(),
            P(),
            P(),
            P(),
            P(),
            P(),
        ),
        out_specs=(
            P(("dp", "tensor"), None),
            P(),
            P(("dp", "tensor"), None),
            P(("tensor", "dp"), None),
            P(("tensor", "dp"), None),
            P(("tensor", "dp"), None),
            P(("tensor", "dp"), None),
            P(("tensor", "dp"), None),
            P(("tensor", "dp"), None),
            P(),
            P(),
            P(),
            P(),
            P(),
            P(),
            P(),
            P(),
            P(),
            P(),
            P(),
            P(),
            P(),
            P(),
        ),
        check_vma=False,
    )
```
